128 devices in a mesh: grid: 8 (over z, core), dom: 16 (over x, y).
Axes of the slice: x: 4, y: 4, z: 4, core: 2. Of those that a mesh axis runs over, the one named last changes fastest.
Arguments:
- nodal: bfloat16 [8, 256, 128, 256], P('grid', 'dom'), may hold values from -6 to 6
- level_gap: int32 [8, 3], replicated, may hold values from 0 to 2
- partner: int32 [8], replicated, may hold values from 0 to 7, as said below
- flags: int32 [8], replicated, may hold values 0 or 1
- coefs: int32 [8], replicated, may hold values from -2 to 2
- owners: int32 [65536, 1], P('dom'), may hold values from 0 to 127; in each aligned block of 4096 rows (0 to 4095, 4096 to 8191, ...) at most 64 rows name the same one
Outputs:
- diff: float32 [8, 256, 128, 256], P('grid', 'dom')
- owned: float32 [128, 16, 64, 128], P(('grid', 'dom'))
The draws below stay inside these ranges and needn't reach their ends.
Inputs may be any that keep to these rules, and one draw needn't show every extreme that they name: partner[g] differs from g in exactly one bit.
All inputs are finite; a program needn't handle non-finite values.
Results may differ from the reference program's by a relative error of at most 0.0065.
Values may be sent and summed in bfloat16 or wider, within the bound.
No kernel may reach another device: no remote copies, remote signals or barrier semaphores. Data moves between devices by JAX's collectives and lax.ppermute only.
A program may use at most 64 MiB of HBM per device.

```python
import math
import jax
import jax.numpy as jnp
import numpy as np
from jax import lax

NY = 128
NZ = 256
GRIDS = 8
NX = 256
NB_DEV = 4096
BLOCKS = 65536
CAP = 64
N_DOM = 16
DEVICES = 128


def draw_partner(key, part):
    bit_count = GRIDS.bit_length() - 1
    flip_bit = jax.random.randint(jax.random.fold_in(key, 17), (GRIDS,), 0, bit_count).astype(jnp.int32)
    grid_ids = jnp.arange(GRIDS, dtype=jnp.int32)
    return jnp.bitwise_xor(grid_ids, jnp.left_shift(jnp.ones_like(flip_bit), flip_bit)).astype(jnp.int32)


def touch_ends(array, key, smallest, high):
    longest = array.shape.index(max(array.shape))
    spots = []
    for shift in (0, 1):
        where = [jax.random.randint(jax.random.fold_in(key, axis), (), 0, length) for axis, length in enumerate(array.shape)]
        where[longest] = (where[longest] + shift) % array.shape[longest]
        spots.append(tuple(where))
    return array.at[spots[0]].set(smallest).at[spots[1]].set(high)


def levels(own_key, dims, split, low, top_value):
    level = 1.0
    for dim, blocks in split:
        steps = jax.random.uniform(jax.random.fold_in(jax.random.fold_in(own_key, 6), dim), (blocks,), jnp.float32, low / len(split), top_value / len(split))
        level = level * jnp.repeat(jnp.exp(steps), dims[dim] // blocks).reshape((-1,) + (1,) * (len(dims) - 1 - dim))
    return level


def shared_out(key, own, number, rows, number_of, top, bound, skew):
    order = jax.random.permutation(key, number_of)
    packed, usual = shares(number_of, rows * top, bound, skew, True), shares(number_of, rows * top, bound, skew, False)
    places = jnp.arange(number_of)

    def named(sizes, turn):
        used = int((sizes > 0).sum())
        fixed = max(1, used // 4)
        moved = fixed + (places - fixed + turn * (used - fixed)) % max(1, number_of - fixed)
        return jnp.zeros((number_of,), jnp.int32).at[order[jnp.where(places < fixed, places, moved)]].set(jnp.asarray(sizes, jnp.int32))

    sizes = jnp.where(number % 4 == 0, named(packed, number // 4), named(usual, number - number // 4 - 1))
    mixed = jax.random.permutation(jax.random.fold_in(own, 3), number_of)
    giver, receiver = mixed[0:number_of // 2 * 2:2], mixed[1:number_of // 2 * 2:2]
    slack = jnp.minimum(sizes[giver] - 1, bound - sizes[receiver]) // 2
    slack = jnp.where((giver == order[0]) | (receiver == order[0]) | (sizes[receiver] == 0), 0, jnp.maximum(slack, 0))
    moved = jax.random.randint(jax.random.fold_in(own, 4), (number_of // 2,), 0, 1 << 20) % (slack + 1)
    sizes = sizes.at[giver].add(-moved).at[receiver].add(moved)
    labels = jnp.searchsorted(jnp.cumsum(sizes), jnp.arange(rows * top), side="right").astype(jnp.int32)
    grid = labels.reshape(top, rows).T
    grid = grid[jax.random.permutation(jax.random.fold_in(own, 1), rows)]
    turn = jax.random.randint(jax.random.fold_in(own, 2), (rows, 1), 0, top)
    return jnp.take_along_axis(grid, (jnp.arange(top)[None, :] + turn) % top, axis=1)


def shares(number_of, total, reach, lean, full):
    loads = [(1 << 20) // math.isqrt(grade ** lean) + 1 for grade in range(1, number_of + 1)]
    largest = reach if full else min(reach, max(-(-total // number_of), total * loads[0] // sum(loads)))
    least = 1 if total - largest >= number_of - 1 else 0
    holding, spare = [largest] + [least] * (number_of - 1), total - largest - least * (number_of - 1)
    while spare > 0:
        candidates = [i for i in range(1, number_of) if holding[i] < largest] or [i for i in range(1, number_of) if holding[i] < reach]
        whole, left = sum([loads[i] for i in candidates]), spare
        for i in candidates:
            more = min(reach - holding[i], max(1, left * loads[i] // whole), spare)
            holding[i] = holding[i] + more
            spare = spare - more
    return np.array(holding)


def centred(own_key, extent, width, most, pieces=(), kind=jnp.bfloat16):
    drawn = width * jax.random.normal(own_key, extent, jnp.float32)
    if pieces:
        drawn = drawn * levels(own_key, extent, pieces, -0.22, 0.18)
    return jnp.clip(drawn, -most, most).astype(kind)


def setup_inputs(seed: int = 0) -> dict:
    key_list = jax.random.split(jax.random.key(seed), 7)
    nodal = centred(key_list[0], (GRIDS, NX, NY, NZ), 1.0, 6.0, ((0, 8), (1, 16)))
    level_gap = touch_ends(jax.random.randint(key_list[1], (GRIDS, 3), 0, 3), jax.random.fold_in(key_list[1], 1), 0, 2).astype(jnp.int32)
    partner = draw_partner(jax.random.fold_in(key_list[6], 71), 0)
    flags = touch_ends((jax.random.randint(key_list[3], (GRIDS,), 0, 4) < 1).astype(jnp.int32), jax.random.fold_in(key_list[3], 1), 0, 1)
    coefs = touch_ends(jax.random.randint(key_list[4], (GRIDS,), -2, 3), jax.random.fold_in(key_list[4], 1), -2, 2).astype(jnp.int32)
    owners_keys = jax.random.split(jax.random.fold_in(key_list[5], 1), BLOCKS // NB_DEV)
    owners_turns = jax.random.permutation(jax.random.fold_in(key_list[5], 3), BLOCKS // NB_DEV)
    owners = jax.vmap(lambda own, number: shared_out(jax.random.fold_in(key_list[5], 2), own, number, NB_DEV, DEVICES, 1, CAP, 1))(owners_keys, owners_turns).reshape((BLOCKS, 1))
    return dict(nodal=nodal, level_gap=level_gap, partner=partner, flags=flags, coefs=coefs, owners=owners)


HIGH = lax.Precision.HIGHEST


def lowbit(positions):
    return jnp.bitwise_and(positions, -positions)


def hier_matrix(length):
    positions = jnp.arange(1, length + 1, dtype=jnp.int32)
    lowest = lowbit(positions)
    source = positions[:, None]
    identity = (source == positions[None, :]).astype(jnp.float32)
    below_hit = (source == (positions - lowest)[None, :]).astype(jnp.float32)
    above_hit = (source == (positions + lowest)[None, :]).astype(jnp.float32)
    return identity - 0.5 * below_hit - 0.5 * above_hit


def keep_level(positions, gap_value):
    return lowbit(positions) >= jnp.left_shift(jnp.ones_like(gap_value), gap_value)


def masked(values, level_gaps, x_pos, y_pos, z_pos):
    keep_all = keep_level(x_pos, level_gaps[0])[:, None, None]
    keep_all = keep_all & keep_level(y_pos, level_gaps[1])[None, :, None]
    keep_all = keep_all & keep_level(z_pos, level_gaps[2])[None, None, :]
    return jnp.where(keep_all, values, jnp.float32(0.0))


def yz_levels(values, y_matrix, z_matrix):
    result = jnp.einsum('xqz,qp->xpz', values, y_matrix, precision=HIGH)
    shape = result.shape
    result = jnp.dot(result.reshape(-1, shape[2]), z_matrix, precision=HIGH)
    return result.reshape(shape)


def x_levels(values, x_pos):
    length = values.shape[0]
    padded = jnp.pad(values, ((4, 4), (0, 0), (0, 0)))
    lowest = lowbit(x_pos)
    result = values
    for stride in (1, 2, 4):
        below_rows = padded[4 - stride:4 - stride + length]
        above_rows = padded[4 + stride:4 + stride + length]
        result = jnp.where((lowest == stride)[:, None, None], values - 0.5 * (below_rows + above_rows), result)
    return result


def reference(nodal, level_gap, partner, flags, coefs, owners):
    y_matrix = hier_matrix(NY)
    z_matrix = hier_matrix(NZ)
    x_pos = jnp.arange(5, NX + 5, dtype=jnp.int32)
    y_pos = jnp.arange(1, NY + 1, dtype=jnp.int32)
    z_pos = jnp.arange(1, NZ + 1, dtype=jnp.int32)
    surplus_list = []
    for g in range(GRIDS):
        values = x_levels(nodal[g].astype(jnp.float32), x_pos)
        values = yz_levels(values, y_matrix, z_matrix)
        surplus_list.append(masked(values, level_gap[g], x_pos, y_pos, z_pos).astype(jnp.bfloat16))
    surplus = jnp.stack(surplus_list)
    diff_list = []
    for g in range(GRIDS):
        partner_index = partner[g]
        level_gaps = jnp.maximum(level_gap[g], level_gap[partner_index])
        theirs = lax.dynamic_index_in_dim(surplus, partner_index, 0, keepdims=False)
        delta = surplus[g].astype(jnp.float32) - theirs.astype(jnp.float32)
        diff_list.append(masked(delta, level_gaps, x_pos, y_pos, z_pos))
    diff = jnp.stack(diff_list)
    weights = coefs.astype(jnp.float32) * (1 - flags).astype(jnp.float32)
    combined = jnp.einsum('g,gxyz->xyz', weights, surplus.astype(jnp.float32), precision=HIGH)
    block_rows = combined.reshape(N_DOM, NB_DEV, 128)
    owner_ids = owners.reshape(N_DOM, NB_DEV)

    def place(rows_shard, owner_shard):
        one_hot = (owner_shard[:, None] == jnp.arange(DEVICES, dtype=jnp.int32)[None, :]).astype(jnp.int32)
        earlier = jnp.cumsum(one_hot, axis=0, dtype=jnp.int32) - one_hot
        slot_index = jnp.sum(earlier * one_hot, axis=1, dtype=jnp.int32)
        return jnp.zeros((DEVICES, CAP, 128), jnp.float32).at[owner_shard, slot_index].set(rows_shard)

    placed = jax.vmap(place)(block_rows, owner_ids)
    owned = jnp.transpose(placed, (1, 0, 2, 3))
    return diff, owned
```

```python
import jax
import jax.numpy as jnp
import numpy as np
from jax import lax
from jax.experimental import pallas as pl
from jax.experimental.pallas import tpu as pltpu
from jax.sharding import PartitionSpec as P

F32 = jnp.float32
BF16 = jnp.bfloat16
PIECES = ((14, 15, 0, 1), (2, 3, 4, 5), (6, 7, 8, 9), (10, 11, 12, 13))


def hier_matrix(length):
    pos = np.arange(1, length + 1)
    low = pos & -pos
    source = pos[:, None]
    return (
        (source == pos[None, :]) * 1.0
        - 0.5 * (source == (pos - low)[None, :])
        - 0.5 * (source == (pos + low)[None, :])
    ).astype(np.float32)


def vmem():
    return pl.BlockSpec(memory_space=pltpu.VMEM)


def smem():
    return pl.BlockSpec(memory_space=pltpu.SMEM)


def shape(dims, dtype):
    return jax.ShapeDtypeStruct(dims, dtype)


def params():
    return pltpu.CompilerParams(vmem_limit_bytes=48 * 1024 * 1024)


def cost(flops, nbytes):
    return pl.CostEstimate(flops=flops, bytes_accessed=nbytes, transcendentals=0)


def kept(iota_pos, gap):
    return (iota_pos & ((1 << gap) - 1)) == 0


def split2(w):
    high = w.astype(BF16)
    return high, (w - high.astype(F32)).astype(BF16)


def hier_rows(rows, field, below, above, gap_ref, ymat_ref, zmat_ref, store):
    group = lax.axis_index("grid")
    domain = lax.axis_index("dom")
    gx, gy, gz = gap_ref[group, 0], gap_ref[group, 1], gap_ref[group, 2]
    ny, nz = ymat_ref.shape[0], zmat_ref.shape[0]
    keep_y = kept(lax.broadcasted_iota(jnp.int32, (ny, ny), 0) + 1, gy)
    keep_z = kept(lax.broadcasted_iota(jnp.int32, (nz, nz), 1) + 1, gz)
    ym = jnp.where(keep_y, ymat_ref[...], 0.0).astype(BF16)
    zm = jnp.where(keep_z, zmat_ref[...], 0.0).astype(BF16)
    yy = jnp.concatenate([ym, ym], axis=1)

    def layer(i):
        if i < 0:
            return below()
        if i > 15:
            return above()
        return field(i)

    for i in rows:
        pos = domain * 16 + (i + 5)
        low = (i + 5) & -(i + 5)
        w = layer(i)
        if low <= 4:
            w = w - 0.5 * (layer(i - low) + layer(i + low))
        w = w * jnp.where(kept(pos, gx), 1.0, 0.0)
        high, rest = split2(w)
        u = jnp.dot(yy, jnp.concatenate([high, rest], axis=0), preferred_element_type=F32)
        high, rest = split2(u)
        v = jnp.dot(high, zm, preferred_element_type=F32)
        v = v + jnp.dot(rest, zm, preferred_element_type=F32)
        store(i, v.astype(BF16))


def early_kernel(gap_ref, field_ref, ymat_ref, zmat_ref, *outs):
    def store(i, value):
        outs[(i - 2) // 4][(i - 2) % 4] = value

    hier_rows(
        range(2, 14), lambda i: field_ref[0, i].astype(F32), None, None,
        gap_ref, ymat_ref, zmat_ref, store,
    )


def late_kernel(gap_ref, field_ref, one_ref, two_ref, ymat_ref, zmat_ref, out_ref):
    odd = (lax.axis_index("dom") % 2).astype(F32)
    even = 1.0 - odd

    def below():
        return one_ref[0].astype(F32) * odd + two_ref[0].astype(F32) * even

    def above():
        return one_ref[0].astype(F32) * even + two_ref[0].astype(F32) * odd

    def store(i, value):
        out_ref[PIECES[0].index(i)] = value

    hier_rows(
        PIECES[0], lambda i: field_ref[0, i].astype(F32), below, above,
        gap_ref, ymat_ref, zmat_ref, store,
    )


def slots_kernel(owner_ref, dest_ref):
    group = lax.axis_index("grid")
    n = 256
    before = (
        lax.broadcasted_iota(jnp.int32, (n, n), 0) < lax.broadcasted_iota(jnp.int32, (n, n), 1)
    ).astype(BF16)
    ids = lax.broadcasted_iota(jnp.int32, (128, n), 0)
    count = jnp.zeros((128, 1), F32)
    for r in range(16):
        owner = owner_ref[r : r + 1, :]
        hit = ids == owner
        one_hot = hit.astype(F32)
        earlier = jnp.dot(one_hot.astype(BF16), before, preferred_element_type=F32) + count
        slot = jnp.sum(one_hot * earlier, axis=0, keepdims=True).astype(jnp.int32)
        count = count + jnp.sum(one_hot, axis=1, keepdims=True)
        apart = (owner >> 5) ^ (group >> 1)
        row = (apart * 16 + (owner & 15)) * 64 + slot
        dest_ref[r : r + 1, :] = jnp.where(((owner >> 4) & 1) == (group & 1), row, 4096)


def place_kernel(dest_ref, flag_ref, coef_ref, *refs):
    own, other = refs[0:4], refs[4:8]
    outs = refs[8:12]
    low_ref, high_ref, packed = refs[12:15]
    group = lax.axis_index("grid")
    w0 = (coef_ref[group] * (1 - flag_ref[group])).astype(F32)
    w1 = (coef_ref[group ^ 1] * (1 - flag_ref[group ^ 1])).astype(F32)
    for q in range(4):
        for j in range(4):
            p = w0 * own[q][j].astype(F32) + w1 * other[q][j].astype(F32)
            i = PIECES[q][j]
            low_ref[pl.ds(i * 128, 128), :] = p[:, 0:128]
            high_ref[pl.ds(i * 128, 128), :] = p[:, 128:256]
    packed[...] = jnp.zeros_like(packed)

    def step(t, carry):
        x = t // 8
        y0 = pl.multiple_of((t % 8) * 16, 16)
        base = pl.multiple_of(t * 16, 16)
        for u in range(16):
            packed[pl.ds(dest_ref[x, (y0 + u) * 2], 1), :] = low_ref[pl.ds(base + u, 1), :]
            packed[pl.ds(dest_ref[x, (y0 + u) * 2 + 1], 1), :] = high_ref[pl.ds(base + u, 1), :]
        return carry

    lax.fori_loop(0, 128, step, 0)
    for q in range(4):
        outs[q][...] = packed[pl.ds(q * 1024, 1024), :].astype(BF16).reshape(16, 64, 128)


def route_kernel(partner_ref, r0, r1, r2, r3, m1, m2, m3):
    group = lax.axis_index("grid")
    held = (r0, r1, r2, r3)
    for m, out in ((1, m1), (2, m2), (3, m3)):
        target = group ^ (2 * m)
        far = ((partner_ref[target] ^ target) >> 1) == 2

        @pl.when(far)
        def _():
            out[...] = held[m ^ 2][...]

        @pl.when(jnp.logical_not(far))
        def _():
            out[...] = held[m ^ 1][...]


def diff_kernel(gap_ref, partner_ref, *refs):
    own, core, near, far = refs[0:4], refs[4:8], refs[8:12], refs[12:16]
    out_ref = refs[16]
    group = lax.axis_index("grid")
    domain = lax.axis_index("dom")
    other = partner_ref[group]
    gx, gy, gz = (jnp.maximum(gap_ref[group, k], gap_ref[other, k]) for k in range(3))
    dims = (128, 256)
    keep_y = kept(lax.broadcasted_iota(jnp.int32, dims, 0) + 1, gy)
    keep_z = kept(lax.broadcasted_iota(jnp.int32, dims, 1) + 1, gz)
    keep = jnp.where(keep_y & keep_z, 1.0, 0.0)
    flip = (other ^ group) >> 1
    for kind, theirs in ((0, core), (1, near), (2, far)):

        @pl.when(flip == kind)
        def _():
            for q in range(4):
                for j in range(4):
                    i = PIECES[q][j]
                    here = keep * jnp.where(kept(domain * 16 + (i + 5), gx), 1.0, 0.0)
                    out_ref[0, i] = here * (own[q][j].astype(F32) - theirs[q][j].astype(F32))


def sum_kernel(p0, p1, p2, p3, *outs):
    x = lax.axis_index("dom") // 4
    for b in range(4):
        s = pl.ds((x ^ b) * 4, 4)
        total = (p0[s].astype(F32) + p1[s].astype(F32)) + (p2[s].astype(F32) + p3[s].astype(F32))
        outs[b][...] = total.astype(BF16)


def turn_kernel(e0, e1, e2, e3, *outs):
    y = lax.axis_index("dom") % 4
    for b in range(4):
        for a, e in enumerate((e0, e1, e2, e3)):
            outs[b][a] = e[y ^ b]


def owned_kernel(e0, e1, e2, e3, out_ref):
    domain = lax.axis_index("dom")
    for b, e in enumerate((e0, e1, e2, e3)):
        for a in range(4):
            out_ref[0, domain ^ (a * 4 + b)] = e[a].astype(F32)


def call(kernel, outs, ins, scratch=(), flops=0, nbytes=1 << 20, name=None):
    many = isinstance(outs, (list, tuple))
    return pl.pallas_call(
        kernel,
        out_shape=outs,
        in_specs=ins,
        out_specs=[vmem() for _ in outs] if many else vmem(),
        scratch_shapes=scratch,
        compiler_params=params(),
        cost_estimate=cost(flops, nbytes),
        name=name,
    )


def flipped(value, axis, bits):
    return lax.ppermute(value, axis, [(i, i ^ bits) for i in range(lax.axis_size(axis))])


def body(nodal, level_gap, partner, flags, coefs, owners):
    domain = lax.axis_index("dom")
    odd = domain % 2
    ymat = jnp.asarray(hier_matrix(128).T)
    zmat = jnp.asarray(hier_matrix(256))

    first = lax.dynamic_index_in_dim(nodal[0], 15 - 12 * odd, 0)
    second = lax.dynamic_index_in_dim(nodal[0], 3 + 12 * odd, 0)
    one = flipped(first, "dom", 1)
    two = lax.ppermute(
        second, "dom", [(i, i + 1) for i in range(1, 15, 2)] + [(i + 1, i) for i in range(1, 15, 2)]
    )

    piece = shape((4, 128, 256), BF16)
    early = call(early_kernel, [piece] * 3, [smem(), vmem(), vmem(), vmem()],
                 flops=12 * 6 * 10**7, nbytes=2 << 20, name="early")(level_gap, nodal, ymat, zmat)
    got = [None] + [flipped(early[b - 1], "grid", 2 * b) for b in (1, 2, 3)]
    core = [None] + [flipped(e, "grid", 1) for e in early]

    dest = call(slots_kernel, shape((16, 256), jnp.int32), [vmem()], flops=10**9, name="slots")(
        owners.reshape(16, 256)
    )

    late = call(late_kernel, piece, [smem()] + [vmem()] * 5,
                flops=4 * 6 * 10**7, name="late")(level_gap, nodal, one, two, ymat, zmat)
    own = [late, *early]
    core[0] = flipped(late, "grid", 1)
    got[0] = late

    bundle = shape((16, 64, 128), BF16)
    packed = call(
        place_kernel, [bundle] * 4, [smem()] * 3 + [vmem()] * 8,
        scratch=[pltpu.VMEM((2048, 128), F32), pltpu.VMEM((2048, 128), F32), pltpu.VMEM((4104, 128), F32)],
        flops=10**7, nbytes=16 << 20, name="place",
    )(dest, flags, coefs, *own, *core)
    summed = [packed[0]] + [flipped(packed[b], "grid", 2 * b) for b in (1, 2, 3)]

    sent = call(route_kernel, [piece] * 3, [smem()] + [vmem()] * 4, name="route")(partner, *got)
    came = [None] + [flipped(sent[m - 1], "grid", 2 * m) for m in (1, 2, 3)]

    part = shape((4, 64, 128), BF16)
    by_x = call(sum_kernel, [part] * 4, [vmem()] * 4, name="sum")(*summed)
    by_x = [by_x[0]] + [flipped(by_x[b], "dom", 4 * b) for b in (1, 2, 3)]
    by_y = call(turn_kernel, [part] * 4, [vmem()] * 4, name="turn")(*by_x)
    by_y = [by_y[0]] + [flipped(by_y[b], "dom", b) for b in (1, 2, 3)]
    owned = call(owned_kernel, shape((1, 16, 64, 128), F32), [vmem()] * 4, name="owned")(*by_y)

    near = (came[1], got[1], came[3], came[2])
    far = (came[2], came[3], got[2], came[1])
    diff = call(diff_kernel, shape((1, 16, 128, 256), F32), [smem()] * 2 + [vmem()] * 16,
                nbytes=6 << 20, name="diff")(level_gap, partner, *own, *core, *near, *far)
    return diff, owned


def solution(mesh):
    in_specs = (P("grid", "dom", None, None), P(), P(), P(), P(), P("dom", None))
    out_specs = (P("grid", "dom", None, None), P(("grid", "dom"), None, None, None))
    return jax.shard_map(body, mesh=mesh, in_specs=in_specs, out_specs=out_specs, check_vma=False)
```

```python
import jax
import jax.numpy as jnp
from jax import lax
from jax.experimental import pallas as pl
from jax.experimental.pallas import tpu as pltpu
from jax.sharding import PartitionSpec as P

F32 = jnp.float32
BF16 = jnp.bfloat16
PIECES = ((14, 15, 0, 1), (2, 3, 4, 5), (6, 7, 8, 9), (10, 11, 12, 13))


def hier_matrix(length, out_dim, gap):
    pos = lax.broadcasted_iota(jnp.int32, (length, length), out_dim) + 1
    source = lax.broadcasted_iota(jnp.int32, (length, length), 1 - out_dim) + 1
    low = pos & -pos
    away = jnp.abs(source - pos)
    value = jnp.where(away == 0, 1.0, jnp.where(away == low, -0.5, 0.0))
    return jnp.where(kept(pos, gap), value, 0.0).astype(BF16)


def vmem():
    return pl.BlockSpec(memory_space=pltpu.VMEM)


def smem():
    return pl.BlockSpec(memory_space=pltpu.SMEM)


def shape(dims, dtype):
    return jax.ShapeDtypeStruct(dims, dtype)


def params():
    return pltpu.CompilerParams(vmem_limit_bytes=48 * 1024 * 1024)


def cost(flops, nbytes):
    return pl.CostEstimate(flops=flops, bytes_accessed=nbytes, transcendentals=0)


def kept(iota_pos, gap):
    return (iota_pos & ((1 << gap) - 1)) == 0


def split2(w):
    high = w.astype(BF16)
    return high, (w - high.astype(F32)).astype(BF16)


def hier_rows(rows, field, below, above, gap_ref, store):
    group = lax.axis_index("grid")
    domain = lax.axis_index("dom")
    gx, gy, gz = gap_ref[0, group], gap_ref[1, group], gap_ref[2, group]
    ym = hier_matrix(128, 0, gy)
    zm = hier_matrix(256, 1, gz)
    yy = jnp.concatenate([ym, ym], axis=1)

    def layer(i):
        if i < 0:
            return below()
        if i > 15:
            return above()
        return field(i)

    for i in rows:
        pos = domain * 16 + (i + 5)
        low = (i + 5) & -(i + 5)
        w = layer(i)
        if low <= 4:
            w = w - 0.5 * (layer(i - low) + layer(i + low))
        w = w * jnp.where(kept(pos, gx), 1.0, 0.0)
        high, rest = split2(w)
        u = jnp.dot(yy, jnp.concatenate([high, rest], axis=0), preferred_element_type=F32)
        high, rest = split2(u)
        v = jnp.dot(high, zm, preferred_element_type=F32)
        v = v + jnp.dot(rest, zm, preferred_element_type=F32)
        store(i, v.astype(BF16))


def early_kernel(gap_ref, field_ref, all_ref, *outs):
    def store(i, value):
        outs[(i - 2) // 4][(i - 2) % 4] = value
        all_ref[i - 2] = value

    hier_rows(range(2, 14), lambda i: field_ref[0, i].astype(F32), None, None, gap_ref, store)


def late_kernel(gap_ref, field_ref, one_ref, two_ref, out_ref):
    odd = (lax.axis_index("dom") % 2).astype(F32)
    even = 1.0 - odd

    def below():
        return one_ref[0].astype(F32) * odd + two_ref[0].astype(F32) * even

    def above():
        return one_ref[0].astype(F32) * even + two_ref[0].astype(F32) * odd

    def store(i, value):
        out_ref[PIECES[0].index(i)] = value

    hier_rows(PIECES[0], lambda i: field_ref[0, i].astype(F32), below, above, gap_ref, store)


def slots_kernel(owner_ref, dest_ref):
    group = lax.axis_index("grid")
    n = 256
    before = (
        lax.broadcasted_iota(jnp.int32, (n, n), 0) < lax.broadcasted_iota(jnp.int32, (n, n), 1)
    ).astype(BF16)
    ids = lax.broadcasted_iota(jnp.int32, (128, n), 0)
    count = jnp.zeros((128, 1), F32)
    for r in range(16):
        owner = jnp.concatenate([owner_ref[k : k + 1, :] for k in (2 * r, 2 * r + 1)], axis=1)
        hit = ids == owner
        one_hot = hit.astype(F32)
        earlier = jnp.dot(one_hot.astype(BF16), before, preferred_element_type=F32) + count
        slot = jnp.sum(one_hot * earlier, axis=0, keepdims=True).astype(jnp.int32)
        count = count + jnp.sum(one_hot, axis=1, keepdims=True)
        apart = (owner >> 5) ^ (group >> 1)
        row = (apart * 16 + (owner & 15)) * 64 + slot
        row = jnp.where(((owner >> 4) & 1) == (group & 1), row, 4096)
        dest_ref[2 * r : 2 * r + 1, :] = row[:, 0:128]
        dest_ref[2 * r + 1 : 2 * r + 2, :] = row[:, 128:256]


def place_kernel(dest_ref, flag_ref, coef_ref, own_late, own_early, core_late, core_early, *refs):
    outs = refs[0:4]
    low_ref, high_ref, packed = refs[4:7]
    group = lax.axis_index("grid")
    w0 = (coef_ref[group] * (1 - flag_ref[group])).astype(F32)
    w1 = (coef_ref[group ^ 1] * (1 - flag_ref[group ^ 1])).astype(F32)

    def add(i, own, core):
        p = w0 * own.astype(F32) + w1 * core.astype(F32)
        low_ref[pl.ds(i * 128, 128), :] = p[:, 0:128]
        high_ref[pl.ds(i * 128, 128), :] = p[:, 128:256]

    for j, i in enumerate(PIECES[0]):
        add(i, own_late[j], core_late[j])
    for i in range(2, 14):
        add(i, own_early[i - 2], core_early[i - 2])
    packed[...] = jnp.zeros_like(packed)

    def step(t, carry):
        base = pl.multiple_of(t * 64, 64)
        for u in range(64):
            packed[pl.ds(dest_ref[2 * base + 2 * u], 1), :] = low_ref[pl.ds(base + u, 1), :]
            packed[pl.ds(dest_ref[2 * base + 2 * u + 1], 1), :] = high_ref[pl.ds(base + u, 1), :]
        return carry

    lax.fori_loop(0, 32, step, 0)
    for q in range(4):
        outs[q][...] = packed[pl.ds(q * 1024, 1024), :].astype(BF16).reshape(16, 64, 128)


def route_kernel(partner_ref, r0, r1, r2, r3, m1, m2, m3):
    group = lax.axis_index("grid")
    held = (r0, r1, r2, r3)
    for m, out in ((1, m1), (2, m2), (3, m3)):
        target = group ^ (2 * m)
        far = ((partner_ref[target] ^ target) >> 1) == 2

        @pl.when(far)
        def _():
            out[...] = held[m ^ 2][...]

        @pl.when(jnp.logical_not(far))
        def _():
            out[...] = held[m ^ 1][...]


def diff_kernel(gap_ref, partner_ref, own_late, own_early, core_late, core_early, *refs):
    near, far = refs[0:4], refs[4:8]
    out_ref = refs[8]
    group = lax.axis_index("grid")
    domain = lax.axis_index("dom")
    other = partner_ref[group]
    gx, gy, gz = (jnp.maximum(gap_ref[k, group], gap_ref[k, other]) for k in range(3))
    dims = (128, 256)
    keep_y = kept(lax.broadcasted_iota(jnp.int32, dims, 0) + 1, gy)
    keep_z = kept(lax.broadcasted_iota(jnp.int32, dims, 1) + 1, gz)
    keep = jnp.where(keep_y & keep_z, 1.0, 0.0)
    flip = (other ^ group) >> 1

    def write(theirs):
        for q in range(4):
            for j, i in enumerate(PIECES[q]):
                own = own_early[i - 2] if q else own_late[j]
                here = keep * jnp.where(kept(domain * 16 + (i + 5), gx), 1.0, 0.0)
                out_ref[0, i] = here * (own.astype(F32) - theirs(q, j, i).astype(F32))

    @pl.when(flip == 0)
    def _():
        write(lambda q, j, i: core_early[i - 2] if q else core_late[j])

    @pl.when(flip == 1)
    def _():
        write(lambda q, j, i: near[q][j])

    @pl.when(flip == 2)
    def _():
        write(lambda q, j, i: far[q][j])


def sum_kernel(p0, p1, p2, p3, *outs):
    x = lax.axis_index("dom") // 4
    for b in range(4):
        s = pl.ds((x ^ b) * 4, 4)
        total = (p0[s].astype(F32) + p1[s].astype(F32)) + (p2[s].astype(F32) + p3[s].astype(F32))
        outs[b][...] = total.astype(BF16)


def turn_kernel(e0, e1, e2, e3, *outs):
    y = lax.axis_index("dom") % 4
    for b in range(4):
        for a, e in enumerate((e0, e1, e2, e3)):
            outs[b][a] = e[y ^ b]


def owned_kernel(e0, e1, e2, e3, out_ref):
    domain = lax.axis_index("dom")
    for b, e in enumerate((e0, e1, e2, e3)):
        for a in range(4):
            out_ref[0, domain ^ (a * 4 + b)] = e[a].astype(F32)


def call(kernel, outs, ins, scratch=(), flops=0, nbytes=1 << 20, name=None):
    many = isinstance(outs, (list, tuple))
    return pl.pallas_call(
        kernel,
        out_shape=outs,
        in_specs=ins,
        out_specs=[vmem() for _ in outs] if many else vmem(),
        scratch_shapes=scratch,
        compiler_params=params(),
        cost_estimate=cost(flops, nbytes),
        name=name,
    )


def flipped(value, axis, bits):
    return lax.ppermute(value, axis, [(i, i ^ bits) for i in range(lax.axis_size(axis))])


def body(nodal, level_gap, partner, flags, coefs, owners):
    domain = lax.axis_index("dom")
    odd = domain % 2
    gaps = level_gap.T

    first = lax.dynamic_index_in_dim(nodal[0], 15 - 12 * odd, 0)
    second = lax.dynamic_index_in_dim(nodal[0], 3 + 12 * odd, 0)
    nodal, first, second = lax.optimization_barrier((nodal, first, second))
    one = flipped(first, "dom", 1)
    two = lax.ppermute(
        second, "dom", [(i, i + 1) for i in range(1, 15, 2)] + [(i + 1, i) for i in range(1, 15, 2)]
    )

    piece = shape((4, 128, 256), BF16)
    inner = shape((12, 128, 256), BF16)
    early, *pieces = call(early_kernel, [inner] + [piece] * 3, [smem(), vmem()],
                          flops=10**9, nbytes=2 << 20, name="early")(gaps, nodal)
    early, one, two = lax.optimization_barrier((early, one, two))
    core_early = flipped(early, "grid", 1)
    dest = call(slots_kernel, shape((32, 128), jnp.int32), [vmem()], flops=10**9, name="slots")(
        owners.reshape(32, 128)
    ).reshape(4096)
    late = call(late_kernel, piece, [smem()] + [vmem()] * 3,
                flops=10**9, name="late")(gaps, nodal, one, two)
    core_late = flipped(late, "grid", 1)
    got = [late] + [flipped(pieces[b - 1], "grid", 2 * b) for b in (1, 2, 3)]
    held = (late, early, core_late, core_early)

    bundle = shape((16, 64, 128), BF16)
    packed = call(
        place_kernel, [bundle] * 4, [smem()] * 3 + [vmem()] * 4,
        scratch=[pltpu.VMEM((2048, 128), F32), pltpu.VMEM((2048, 128), F32), pltpu.VMEM((4104, 128), F32)],
        flops=10**7, nbytes=16 << 20, name="place",
    )(dest, flags, coefs, *held)
    summed = [packed[0]] + [flipped(packed[b], "grid", 2 * b) for b in (1, 2, 3)]

    sent = call(route_kernel, [piece] * 3, [smem()] + [vmem()] * 4, name="route")(partner, *got)
    came = [None] + [flipped(sent[m - 1], "grid", 2 * m) for m in (1, 2, 3)]

    part = shape((4, 64, 128), BF16)
    by_x = call(sum_kernel, [part] * 4, [vmem()] * 4, name="sum")(*summed)
    by_x = [by_x[0]] + [flipped(by_x[b], "dom", 4 * b) for b in (1, 2, 3)]
    by_y = call(turn_kernel, [part] * 4, [vmem()] * 4, name="turn")(*by_x)
    by_y = [by_y[0]] + [flipped(by_y[b], "dom", b) for b in (1, 2, 3)]
    owned = call(owned_kernel, shape((1, 16, 64, 128), F32), [vmem()] * 4, name="owned")(*by_y)

    near = (came[1], got[1], came[3], came[2])
    far = (came[2], came[3], got[2], came[1])
    diff = call(diff_kernel, shape((1, 16, 128, 256), F32), [smem()] * 2 + [vmem()] * 12,
                nbytes=6 << 20, name="diff")(gaps, partner, *held, *near, *far)
    return diff, owned


def solution(mesh):
    in_specs = (P("grid", "dom", None, None), P(), P(), P(), P(), P("dom", None))
    out_specs = (P("grid", "dom", None, None), P(("grid", "dom"), None, None, None))
    return jax.shard_map(body, mesh=mesh, in_specs=in_specs, out_specs=out_specs, check_vma=False)
```

```python
import jax
import jax.numpy as jnp
from jax import lax
from jax.experimental import pallas as pl
from jax.experimental.pallas import tpu as pltpu
from jax.sharding import PartitionSpec as P

F32 = jnp.float32
BF16 = jnp.bfloat16
PIECES = ((14, 15, 0, 1), (2, 3, 4, 5), (6, 7, 8, 9), (10, 11, 12, 13))


def hier_matrix(length, out_dim, gap):
    pos = lax.broadcasted_iota(jnp.int32, (length, length), out_dim) + 1
    source = lax.broadcasted_iota(jnp.int32, (length, length), 1 - out_dim) + 1
    low = pos & -pos
    away = jnp.abs(source - pos)
    value = jnp.where(away == 0, 1.0, jnp.where(away == low, -0.5, 0.0))
    return jnp.where(kept(pos, gap), value, 0.0).astype(BF16)


def vmem():
    return pl.BlockSpec(memory_space=pltpu.VMEM)


def smem():
    return pl.BlockSpec(memory_space=pltpu.SMEM)


def anywhere():
    return pl.BlockSpec(memory_space=pl.ANY)


def shape(dims, dtype):
    return jax.ShapeDtypeStruct(dims, dtype)


def params():
    return pltpu.CompilerParams(vmem_limit_bytes=8 * 1024 * 1024)


def cost(flops, nbytes):
    return pl.CostEstimate(flops=flops, bytes_accessed=nbytes, transcendentals=0)


def kept(iota_pos, gap):
    return (iota_pos & ((1 << gap) - 1)) == 0


def split2(w):
    high = w.astype(BF16)
    return high, (w - high.astype(F32)).astype(BF16)


def hier_rows(rows, field, below, above, gap_ref, store):
    group = lax.axis_index("grid")
    domain = lax.axis_index("dom")
    gx, gy, gz = gap_ref[0, group], gap_ref[1, group], gap_ref[2, group]
    ym = hier_matrix(128, 0, gy)
    zm = hier_matrix(256, 1, gz)
    yy = jnp.concatenate([ym, ym], axis=1)

    def layer(i):
        if i < 0:
            return below()
        if i > 15:
            return above()
        return field(i)

    for i in rows:
        pos = domain * 16 + (i + 5)
        low = (i + 5) & -(i + 5)
        w = layer(i)
        if low <= 4:
            w = w - 0.5 * (layer(i - low) + layer(i + low))
        w = w * jnp.where(kept(pos, gx), 1.0, 0.0)
        high, rest = split2(w)
        u = jnp.dot(yy, jnp.concatenate([high, rest], axis=0), preferred_element_type=F32)
        high, rest = split2(u)
        v = jnp.dot(high, zm, preferred_element_type=F32)
        v = v + jnp.dot(rest, zm, preferred_element_type=F32)
        store(i, v.astype(BF16))


def early_kernel(gap_ref, field_ref, after_ref, all_ref, *outs):
    del after_ref

    def store(i, value):
        outs[(i - 2) // 4][(i - 2) % 4] = value
        all_ref[i - 2] = value

    hier_rows(range(2, 14), lambda i: field_ref[0, i].astype(F32), None, None, gap_ref, store)


def late_kernel(gap_ref, field_ref, one_ref, two_ref, out_ref):
    odd = (lax.axis_index("dom") % 2).astype(F32)
    even = 1.0 - odd

    def below():
        return one_ref[0].astype(F32) * odd + two_ref[0].astype(F32) * even

    def above():
        return one_ref[0].astype(F32) * even + two_ref[0].astype(F32) * odd

    def store(i, value):
        out_ref[PIECES[0].index(i)] = value

    hier_rows(PIECES[0], lambda i: field_ref[0, i].astype(F32), below, above, gap_ref, store)


def slots_kernel(owner_ref, dest_ref):
    group = lax.axis_index("grid")
    n = 256
    before = (
        lax.broadcasted_iota(jnp.int32, (n, n), 0) < lax.broadcasted_iota(jnp.int32, (n, n), 1)
    ).astype(BF16)
    ids = lax.broadcasted_iota(jnp.int32, (128, n), 0)
    count = jnp.zeros((128, 1), F32)
    for r in range(16):
        owner = jnp.concatenate([owner_ref[k : k + 1, :] for k in (2 * r, 2 * r + 1)], axis=1)
        hit = ids == owner
        one_hot = hit.astype(F32)
        earlier = jnp.dot(one_hot.astype(BF16), before, preferred_element_type=F32) + count
        slot = jnp.sum(one_hot * earlier, axis=0, keepdims=True).astype(jnp.int32)
        count = count + jnp.sum(one_hot, axis=1, keepdims=True)
        apart = (owner >> 5) ^ (group >> 1)
        row = (apart * 16 + (owner & 15)) * 64 + slot
        row = jnp.where(((owner >> 4) & 1) == (group & 1), row, 4096)
        dest_ref[2 * r : 2 * r + 1, :] = row[:, 0:128]
        dest_ref[2 * r + 1 : 2 * r + 2, :] = row[:, 128:256]


def place_kernel(dest_ref, flag_ref, coef_ref, own_late, own_early, core_late, core_early, *refs):
    outs = refs[0:4]
    low_ref, high_ref, packed = refs[4:7]
    group = lax.axis_index("grid")
    w0 = (coef_ref[group] * (1 - flag_ref[group])).astype(F32)
    w1 = (coef_ref[group ^ 1] * (1 - flag_ref[group ^ 1])).astype(F32)

    def add(i, own, core):
        p = w0 * own.astype(F32) + w1 * core.astype(F32)
        low_ref[pl.ds(i * 128, 128), :] = p[:, 0:128]
        high_ref[pl.ds(i * 128, 128), :] = p[:, 128:256]

    for j, i in enumerate(PIECES[0]):
        add(i, own_late[j], core_late[j])
    for i in range(2, 14):
        add(i, own_early[i - 2], core_early[i - 2])
    packed[...] = jnp.zeros_like(packed)

    def step(t, carry):
        base = pl.multiple_of(t * 64, 64)
        for u in range(64):
            packed[pl.ds(dest_ref[2 * base + 2 * u], 1), :] = low_ref[pl.ds(base + u, 1), :]
            packed[pl.ds(dest_ref[2 * base + 2 * u + 1], 1), :] = high_ref[pl.ds(base + u, 1), :]
        return carry

    lax.fori_loop(0, 32, step, 0)
    for q in range(4):
        outs[q][...] = packed[pl.ds(q * 1024, 1024), :].astype(BF16).reshape(16, 64, 128)


def route_kernel(partner_ref, r0, r1, r2, r3, m1, m2, m3):
    group = lax.axis_index("grid")
    held = (r0, r1, r2, r3)
    for m, out in ((1, m1), (2, m2), (3, m3)):
        target = group ^ (2 * m)
        far = ((partner_ref[target] ^ target) >> 1) == 2

        @pl.when(far)
        def _():
            out[...] = held[m ^ 2][...]

        @pl.when(jnp.logical_not(far))
        def _():
            out[...] = held[m ^ 1][...]


def diff_kernel(gap_ref, partner_ref, own_late, own_early, core_late, core_early, *refs):
    near, far = refs[0:4], refs[4:8]
    out_ref = refs[8]
    group = lax.axis_index("grid")
    domain = lax.axis_index("dom")
    other = partner_ref[group]
    gx, gy, gz = (jnp.maximum(gap_ref[k, group], gap_ref[k, other]) for k in range(3))
    dims = (128, 256)
    keep_y = kept(lax.broadcasted_iota(jnp.int32, dims, 0) + 1, gy)
    keep_z = kept(lax.broadcasted_iota(jnp.int32, dims, 1) + 1, gz)
    keep = jnp.where(keep_y & keep_z, 1.0, 0.0)
    flip = (other ^ group) >> 1

    def write(theirs):
        for q in range(4):
            for j, i in enumerate(PIECES[q]):
                own = own_early[i - 2] if q else own_late[j]
                here = keep * jnp.where(kept(domain * 16 + (i + 5), gx), 1.0, 0.0)
                out_ref[0, i] = here * (own.astype(F32) - theirs(q, j, i).astype(F32))

    @pl.when(flip == 0)
    def _():
        write(lambda q, j, i: core_early[i - 2] if q else core_late[j])

    @pl.when(flip == 1)
    def _():
        write(lambda q, j, i: near[q][j])

    @pl.when(flip == 2)
    def _():
        write(lambda q, j, i: far[q][j])


def sum_kernel(p0, p1, p2, p3, out_ref):
    total = (p0[...].astype(F32) + p1[...].astype(F32)) + (p2[...].astype(F32) + p3[...].astype(F32))
    out_ref[...] = total.astype(BF16)


def owned_kernel(came_ref, out_ref):
    out_ref[0] = came_ref[...].astype(F32)


def call(kernel, outs, ins, scratch=(), flops=0, nbytes=1 << 20, name=None):
    many = isinstance(outs, (list, tuple))
    return pl.pallas_call(
        kernel,
        out_shape=outs,
        in_specs=ins,
        out_specs=[vmem() for _ in outs] if many else vmem(),
        scratch_shapes=scratch,
        compiler_params=params(),
        cost_estimate=cost(flops, nbytes),
        name=name,
    )


def flipped(value, axis, bits):
    return lax.ppermute(value, axis, [(i, i ^ bits) for i in range(lax.axis_size(axis))])


def body(nodal, level_gap, partner, flags, coefs, owners):
    domain = lax.axis_index("dom")
    odd = domain % 2
    gaps = level_gap.T

    first = lax.dynamic_index_in_dim(nodal[0], 15 - 12 * odd, 0)
    second = lax.dynamic_index_in_dim(nodal[0], 3 + 12 * odd, 0)
    one = flipped(first, "dom", 1)
    two = lax.ppermute(
        second, "dom", [(i, i + 1) for i in range(1, 15, 2)] + [(i + 1, i) for i in range(1, 15, 2)]
    )

    piece = shape((4, 128, 256), BF16)
    inner = shape((12, 128, 256), BF16)
    early, *pieces = call(early_kernel, [inner] + [piece] * 3, [smem(), vmem(), anywhere()],
                          flops=10**9, nbytes=2 << 20, name="early")(gaps, nodal, second)
    early, one, two = lax.optimization_barrier((early, one, two))
    core_early = flipped(early, "grid", 1)
    dest = call(slots_kernel, shape((32, 128), jnp.int32), [vmem()], flops=10**9, name="slots")(
        owners.reshape(32, 128)
    ).reshape(4096)
    late = call(late_kernel, piece, [smem()] + [vmem()] * 3,
                flops=10**9, name="late")(gaps, nodal, one, two)
    core_late = flipped(late, "grid", 1)
    got = [late] + [flipped(pieces[b - 1], "grid", 2 * b) for b in (1, 2, 3)]
    held = (late, early, core_late, core_early)

    bundle = shape((16, 64, 128), BF16)
    packed = call(
        place_kernel, [bundle] * 4, [smem()] * 3 + [vmem()] * 4,
        scratch=[pltpu.VMEM((2048, 128), F32), pltpu.VMEM((2048, 128), F32), pltpu.VMEM((4104, 128), F32)],
        flops=10**7, nbytes=16 << 20, name="place",
    )(dest, flags, coefs, *held)
    summed = [packed[0]] + [flipped(packed[b], "grid", 2 * b) for b in (1, 2, 3)]

    sent = call(route_kernel, [piece] * 3, [smem()] + [vmem()] * 4, name="route")(partner, *got)
    came = [None] + [flipped(sent[m - 1], "grid", 2 * m) for m in (1, 2, 3)]

    total = call(sum_kernel, bundle, [vmem()] * 4, name="sum")(*summed)
    moved = lax.all_to_all(total, "dom", 0, 0, tiled=True)
    owned = call(owned_kernel, shape((1, 16, 64, 128), F32), [vmem()], name="owned")(moved)

    near = (came[1], got[1], came[3], came[2])
    far = (came[2], came[3], got[2], came[1])
    diff = call(diff_kernel, shape((1, 16, 128, 256), F32), [smem()] * 2 + [vmem()] * 12,
                nbytes=6 << 20, name="diff")(gaps, partner, *held, *near, *far)
    return diff, owned


def solution(mesh):
    in_specs = (P("grid", "dom", None, None), P(), P(), P(), P(), P("dom", None))
    out_specs = (P("grid", "dom", None, None), P(("grid", "dom"), None, None, None))
    return jax.shard_map(body, mesh=mesh, in_specs=in_specs, out_specs=out_specs, check_vma=False)
```

```python
import functools

import jax
import jax.numpy as jnp
from jax import lax
from jax.experimental import pallas as pl
from jax.experimental.pallas import tpu as pltpu
from jax.sharding import PartitionSpec as P

F32 = jnp.float32
BF16 = jnp.bfloat16
PIECES = ((14, 15, 0, 1), (2, 3, 4, 5), (6, 7, 8, 9), (10, 11, 12, 13))


def hier_matrix(length, out_dim, gap):
    pos = lax.broadcasted_iota(jnp.int32, (length, length), out_dim) + 1
    source = lax.broadcasted_iota(jnp.int32, (length, length), 1 - out_dim) + 1
    low = pos & -pos
    away = jnp.abs(source - pos)
    value = jnp.where(away == 0, 1.0, jnp.where(away == low, -0.5, 0.0))
    return jnp.where(kept(pos, gap), value, 0.0).astype(BF16)


def vmem():
    return pl.BlockSpec(memory_space=pltpu.VMEM)


def smem():
    return pl.BlockSpec(memory_space=pltpu.SMEM)


def anywhere():
    return pl.BlockSpec(memory_space=pl.ANY)


def shape(dims, dtype):
    return jax.ShapeDtypeStruct(dims, dtype)


def params():
    return pltpu.CompilerParams(vmem_limit_bytes=8 * 1024 * 1024)


def cost(flops, nbytes):
    return pl.CostEstimate(flops=flops, bytes_accessed=nbytes, transcendentals=0)


def kept(iota_pos, gap):
    return (iota_pos & ((1 << gap) - 1)) == 0


def split2(w):
    high = w.astype(BF16)
    return high, (w - high.astype(F32)).astype(BF16)


def hier_rows(rows, field, below, above, gap_ref, store):
    group = lax.axis_index("grid")
    domain = lax.axis_index("dom")
    gx, gy, gz = gap_ref[0, group], gap_ref[1, group], gap_ref[2, group]
    ym = hier_matrix(128, 0, gy)
    zm = hier_matrix(256, 1, gz)
    yy = jnp.concatenate([ym, ym], axis=1)

    def layer(i):
        if i < 0:
            return below()
        if i > 15:
            return above()
        return field(i)

    for i in rows:
        pos = domain * 16 + (i + 5)
        low = (i + 5) & -(i + 5)
        w = layer(i)
        if low <= 4:
            w = w - 0.5 * (layer(i - low) + layer(i + low))
        w = w * jnp.where(kept(pos, gx), 1.0, 0.0)
        high, rest = split2(w)
        u = jnp.dot(yy, jnp.concatenate([high, rest], axis=0), preferred_element_type=F32)
        high, rest = split2(u)
        v = jnp.dot(high, zm, preferred_element_type=F32)
        v = v + jnp.dot(rest, zm, preferred_element_type=F32)
        store(i, v.astype(BF16))


def early_kernel(gap_ref, field_ref, after_ref, all_ref, *outs):
    del after_ref

    def store(i, value):
        if outs:
            outs[(i - 2) // 4][(i - 2) % 4] = value
        all_ref[i - 2] = value

    hier_rows(range(2, 14), lambda i: field_ref[0, i].astype(F32), None, None, gap_ref, store)


def late_kernel(gap_ref, field_ref, one_ref, two_ref, out_ref):
    odd = (lax.axis_index("dom") % 2).astype(F32)
    even = 1.0 - odd

    def below():
        return one_ref[0].astype(F32) * odd + two_ref[0].astype(F32) * even

    def above():
        return one_ref[0].astype(F32) * even + two_ref[0].astype(F32) * odd

    def store(i, value):
        out_ref[PIECES[0].index(i)] = value

    hier_rows(PIECES[0], lambda i: field_ref[0, i].astype(F32), below, above, gap_ref, store)


def slots_kernel(owner_ref, dest_ref):
    group = lax.axis_index("grid")
    n = 256
    before = (
        lax.broadcasted_iota(jnp.int32, (n, n), 0) < lax.broadcasted_iota(jnp.int32, (n, n), 1)
    ).astype(BF16)
    ids = lax.broadcasted_iota(jnp.int32, (128, n), 0)
    count = jnp.zeros((128, 1), F32)
    for r in range(16):
        owner = jnp.concatenate([owner_ref[k : k + 1, :] for k in (2 * r, 2 * r + 1)], axis=1)
        hit = ids == owner
        one_hot = hit.astype(F32)
        earlier = jnp.dot(one_hot.astype(BF16), before, preferred_element_type=F32) + count
        slot = jnp.sum(one_hot * earlier, axis=0, keepdims=True).astype(jnp.int32)
        count = count + jnp.sum(one_hot, axis=1, keepdims=True)
        apart = (owner >> 5) ^ (group >> 1)
        row = (apart * 16 + (owner & 15)) * 64 + slot
        row = jnp.where(((owner >> 4) & 1) == (group & 1), row, 4096)
        dest_ref[2 * r : 2 * r + 1, :] = row[:, 0:128]
        dest_ref[2 * r + 1 : 2 * r + 2, :] = row[:, 128:256]


def place_kernel(dest_ref, flag_ref, coef_ref, own_late, own_early, core_late, core_early, *refs):
    outs = refs[0:4]
    low_ref, high_ref, packed = refs[4:7]
    group = lax.axis_index("grid")
    w0 = (coef_ref[group] * (1 - flag_ref[group])).astype(F32)
    w1 = (coef_ref[group ^ 1] * (1 - flag_ref[group ^ 1])).astype(F32)

    def add(i, own, core):
        p = w0 * own.astype(F32) + w1 * core.astype(F32)
        low_ref[pl.ds(i * 128, 128), :] = p[:, 0:128]
        high_ref[pl.ds(i * 128, 128), :] = p[:, 128:256]

    for j, i in enumerate(PIECES[0]):
        add(i, own_late[j], core_late[j])
    for i in range(2, 14):
        add(i, own_early[i - 2], core_early[i - 2])
    packed[...] = jnp.zeros_like(packed)

    def step(t, carry):
        base = pl.multiple_of(t * 64, 64)
        for u in range(64):
            packed[pl.ds(dest_ref[2 * base + 2 * u], 1), :] = low_ref[pl.ds(base + u, 1), :]
            packed[pl.ds(dest_ref[2 * base + 2 * u + 1], 1), :] = high_ref[pl.ds(base + u, 1), :]
        return carry

    lax.fori_loop(0, 32, step, 0)
    for q in range(4):
        outs[q][...] = packed[pl.ds(q * 1024, 1024), :].astype(BF16).reshape(16, 64, 128)


def reach(gap_ref, group, other):
    gx, gy = (jnp.maximum(gap_ref[k, group], gap_ref[k, other]) for k in (0, 1))
    rx = jnp.minimum(gx, 2)
    ry = jnp.minimum(gy, 2 - rx)
    return rx, ry, 2 - rx - ry


def picks(length, full_dim, part, skip):
    pos = lax.broadcasted_iota(jnp.int32, (length, length), full_dim) + 1
    place = lax.broadcasted_iota(jnp.int32, (length, length), 1 - full_dim) + 1
    hit = place == part * (length >> skip) + (pos >> skip)
    return jnp.where(hit & kept(pos, skip), 1.0, 0.0).astype(BF16)


def pack_kernel(gap_ref, late_ref, early_ref, near_ref, far_ref, field, total):
    group = lax.axis_index("grid")
    for j, i in enumerate(PIECES[0]):
        field[i] = late_ref[j]
    field[2:14] = early_ref[...]
    for m, out_ref in ((1, near_ref), (2, far_ref)):
        rx, ry, rz = reach(gap_ref, group, group ^ (2 * m))
        total[...] = jnp.zeros_like(total)

        def step(n, carry):
            row = ((n + 1) << rx) - 1
            slab = n >> (2 - rx)
            sub = n & ((1 << (2 - rx)) - 1)
            value = jnp.dot(
                field[row], picks(256, 0, sub >> ry, rz), preferred_element_type=F32
            ).astype(BF16)
            total[slab] += jnp.dot(
                picks(128, 1, sub & ((1 << ry) - 1), ry), value, preferred_element_type=F32
            )
            return carry

        lax.fori_loop(0, 16 >> rx, step, 0)
        out_ref[...] = total[...].astype(BF16)


def diff_kernel(gap_ref, partner_ref, own_late, own_early, core_late, core_early, *refs):
    near_ref, far_ref, out_ref = refs
    group = lax.axis_index("grid")
    domain = lax.axis_index("dom")
    other = partner_ref[group]
    gx, gy, gz = (jnp.maximum(gap_ref[k, group], gap_ref[k, other]) for k in range(3))
    dims = (128, 256)
    keep_y = kept(lax.broadcasted_iota(jnp.int32, dims, 0) + 1, gy)
    keep_z = kept(lax.broadcasted_iota(jnp.int32, dims, 1) + 1, gz)
    keep = jnp.where(keep_y & keep_z, 1.0, 0.0)
    flip = (other ^ group) >> 1
    rx, ry, rz = reach(gap_ref, group, other)

    def own(i):
        return own_early[i - 2] if 2 <= i < 14 else own_late[PIECES[0].index(i)]

    def core(i):
        return core_early[i - 2] if 2 <= i < 14 else core_late[PIECES[0].index(i)]

    def unpacked(came_ref):
        def theirs(i):
            n = ((i + 1) >> rx) - 1
            sub = n & ((1 << (2 - rx)) - 1)
            value = jnp.dot(
                picks(128, 0, sub & ((1 << ry) - 1), ry), came_ref[n >> (2 - rx)],
                preferred_element_type=F32,
            ).astype(BF16)
            return jnp.dot(value, picks(256, 1, sub >> ry, rz), preferred_element_type=F32)

        return theirs

    for kind, theirs in ((0, core), (1, unpacked(near_ref)), (2, unpacked(far_ref))):
        for i in range(16):
            here = kept(domain * 16 + (i + 5), gx)

            @pl.when((flip == kind) & here)
            def _():
                out_ref[0, i] = keep * (own(i).astype(F32) - theirs(i).astype(F32))

            @pl.when((flip == kind) & jnp.logical_not(here))
            def _():
                out_ref[0, i] = jnp.zeros(dims, F32)


def route_kernel(partner_ref, r0, r1, r2, r3, m1, m2, m3):
    group = lax.axis_index("grid")
    held = (r0, r1, r2, r3)
    for m, out in ((1, m1), (2, m2), (3, m3)):
        target = group ^ (2 * m)
        far = ((partner_ref[target] ^ target) >> 1) == 2

        @pl.when(far)
        def _():
            out[...] = held[m ^ 2][...]

        @pl.when(jnp.logical_not(far))
        def _():
            out[...] = held[m ^ 1][...]


def relayed_diff_kernel(gap_ref, partner_ref, own_late, own_early, core_late, core_early, *refs):
    near, far = refs[0:4], refs[4:8]
    out_ref = refs[8]
    group = lax.axis_index("grid")
    domain = lax.axis_index("dom")
    other = partner_ref[group]
    gx, gy, gz = (jnp.maximum(gap_ref[k, group], gap_ref[k, other]) for k in range(3))
    dims = (128, 256)
    keep_y = kept(lax.broadcasted_iota(jnp.int32, dims, 0) + 1, gy)
    keep_z = kept(lax.broadcasted_iota(jnp.int32, dims, 1) + 1, gz)
    keep = jnp.where(keep_y & keep_z, 1.0, 0.0)
    flip = (other ^ group) >> 1

    def write(theirs):
        for q in range(4):
            for j, i in enumerate(PIECES[q]):
                own = own_early[i - 2] if q else own_late[j]
                here = keep * jnp.where(kept(domain * 16 + (i + 5), gx), 1.0, 0.0)
                out_ref[0, i] = here * (own.astype(F32) - theirs(q, j, i).astype(F32))

    @pl.when(flip == 0)
    def _():
        write(lambda q, j, i: core_early[i - 2] if q else core_late[j])

    @pl.when(flip == 1)
    def _():
        write(lambda q, j, i: near[q][j])

    @pl.when(flip == 2)
    def _():
        write(lambda q, j, i: far[q][j])


def fits_kernel(gap_ref, partner_ref, fits_ref):
    fits = jnp.int32(1)
    for group in range(8):
        other = partner_ref[group]
        skips = jnp.int32(0)
        for k in range(3):
            skips = skips + jnp.maximum(gap_ref[k, group], gap_ref[k, other])
        fits = jnp.where((other != (group ^ 1)) & (skips < 2), 0, fits)
    fits_ref[0] = fits


def sum_kernel(p0, p1, p2, p3, out_ref):
    total = (p0[...].astype(F32) + p1[...].astype(F32)) + (p2[...].astype(F32) + p3[...].astype(F32))
    out_ref[...] = total.astype(BF16)


def owned_kernel(came_ref, out_ref):
    out_ref[0] = came_ref[...].astype(F32)


def call(kernel, outs, ins, scratch=(), flops=0, nbytes=1 << 20, name=None):
    many = isinstance(outs, (list, tuple))
    return pl.pallas_call(
        kernel,
        out_shape=outs,
        in_specs=ins,
        out_specs=[vmem() for _ in outs] if many else vmem(),
        scratch_shapes=scratch,
        compiler_params=params(),
        cost_estimate=cost(flops, nbytes),
        name=name,
    )


def flipped(value, axis, bits):
    return lax.ppermute(value, axis, [(i, i ^ bits) for i in range(lax.axis_size(axis))])


def program(small, nodal, gaps, partner, flags, coefs, owners):
    odd = lax.axis_index("dom") % 2

    first = lax.dynamic_index_in_dim(nodal[0], 15 - 12 * odd, 0)
    second = lax.dynamic_index_in_dim(nodal[0], 3 + 12 * odd, 0)
    one = flipped(first, "dom", 1)
    two = lax.ppermute(
        second, "dom", [(i, i + 1) for i in range(1, 15, 2)] + [(i + 1, i) for i in range(1, 15, 2)]
    )

    piece = shape((4, 128, 256), BF16)
    inner = shape((12, 128, 256), BF16)
    early, *pieces = call(
        early_kernel, [inner] + [piece] * (0 if small else 3), [smem(), vmem(), anywhere()],
        flops=10**9, nbytes=2 << 20, name="early",
    )(gaps, nodal, second)
    early, one, two = lax.optimization_barrier((early, one, two))
    core_early = flipped(early, "grid", 1)
    dest = call(slots_kernel, shape((32, 128), jnp.int32), [vmem()], flops=10**9, name="slots")(
        owners.reshape(32, 128)
    ).reshape(4096)
    late = call(late_kernel, piece, [smem()] + [vmem()] * 3,
                flops=10**9, name="late")(gaps, nodal, one, two)
    core_late = flipped(late, "grid", 1)
    held = (late, early, core_late, core_early)

    bundle = shape((16, 64, 128), BF16)
    packed = call(
        place_kernel, [bundle] * 4, [smem()] * 3 + [vmem()] * 4,
        scratch=[pltpu.VMEM((2048, 128), F32), pltpu.VMEM((2048, 128), F32), pltpu.VMEM((4104, 128), F32)],
        flops=10**7, nbytes=16 << 20, name="place",
    )(dest, flags, coefs, *held)
    summed = [packed[0]] + [flipped(packed[b], "grid", 2 * b) for b in (1, 2, 3)]

    if small:
        near, far = call(
            pack_kernel, [piece] * 2, [smem(), vmem(), vmem()],
            scratch=[pltpu.VMEM((16, 128, 256), BF16), pltpu.VMEM((4, 128, 256), F32)],
            flops=10**9, nbytes=2 << 20, name="pack",
        )(gaps, late, early)
        theirs = (flipped(near, "grid", 2), flipped(far, "grid", 4))
    else:
        got = [late] + [flipped(pieces[b - 1], "grid", 2 * b) for b in (1, 2, 3)]
        sent = call(route_kernel, [piece] * 3, [smem()] + [vmem()] * 4, name="route")(partner, *got)
        came = [None] + [flipped(sent[m - 1], "grid", 2 * m) for m in (1, 2, 3)]
        theirs = (came[1], got[1], came[3], came[2], came[2], came[3], got[2], came[1])

    total = call(sum_kernel, bundle, [vmem()] * 4, name="sum")(*summed)
    moved = lax.all_to_all(total, "dom", 0, 0, tiled=True)
    owned = call(owned_kernel, shape((1, 16, 64, 128), F32), [vmem()], name="owned")(moved)

    diff = call(
        diff_kernel if small else relayed_diff_kernel, shape((1, 16, 128, 256), F32),
        [smem()] * 2 + [vmem()] * (4 + len(theirs)), nbytes=6 << 20, name="diff",
    )(gaps, partner, *held, *theirs)
    return diff, owned


def body(nodal, level_gap, partner, flags, coefs, owners):
    gaps = level_gap.T
    fits = pl.pallas_call(
        fits_kernel,
        out_shape=shape((1,), jnp.int32),
        in_specs=[smem(), smem()],
        out_specs=smem(),
        name="fits",
    )(gaps, partner)
    return lax.cond(
        fits[0] != 0,
        functools.partial(program, True),
        functools.partial(program, False),
        nodal, gaps, partner, flags, coefs, owners,
    )


def solution(mesh):
    in_specs = (P("grid", "dom", None, None), P(), P(), P(), P(), P("dom", None))
    out_specs = (P("grid", "dom", None, None), P(("grid", "dom"), None, None, None))
    return jax.shard_map(body, mesh=mesh, in_specs=in_specs, out_specs=out_specs, check_vma=False)
```

```python
import functools

import jax
import jax.numpy as jnp
from jax import lax
from jax.experimental import pallas as pl
from jax.experimental.pallas import tpu as pltpu
from jax.sharding import PartitionSpec as P

F32 = jnp.float32
BF16 = jnp.bfloat16
ORDER = [15, 14, 13, 12, 11, 10, 9, 8, 7, 6, 5, 4, 3, 2, 1, 0]
PIECES = ((14, 15, 0, 1), (2, 3, 4, 5), (6, 7, 8, 9), (10, 11, 12, 13))


def hier_matrix(length, out_dim, gap):
    pos = lax.broadcasted_iota(jnp.int32, (length, length), out_dim) + 1
    source = lax.broadcasted_iota(jnp.int32, (length, length), 1 - out_dim) + 1
    low = pos & -pos
    away = jnp.abs(source - pos)
    value = jnp.where(away == 0, 1.0, jnp.where(away == low, -0.5, 0.0))
    return jnp.where(kept(pos, gap), value, 0.0).astype(BF16)


def vmem():
    return pl.BlockSpec(memory_space=pltpu.VMEM)


def smem():
    return pl.BlockSpec(memory_space=pltpu.SMEM)


def anywhere():
    return pl.BlockSpec(memory_space=pltpu.HBM)


def shape(dims, dtype):
    return jax.ShapeDtypeStruct(dims, dtype)


def params():
    return pltpu.CompilerParams(vmem_limit_bytes=8 * 1024 * 1024)


def cost(flops, nbytes):
    return pl.CostEstimate(flops=flops, bytes_accessed=nbytes, transcendentals=0)


def kept(iota_pos, gap):
    return (iota_pos & ((1 << gap) - 1)) == 0


def split2(w):
    high = w.astype(BF16)
    return high, (w - high.astype(F32)).astype(BF16)


def hier_rows(rows, field, below, above, gap_ref, store):
    group = lax.axis_index("grid")
    domain = lax.axis_index("dom")
    gx, gy, gz = gap_ref[0, group], gap_ref[1, group], gap_ref[2, group]
    ym = hier_matrix(128, 0, gy)
    zm = hier_matrix(256, 1, gz)
    yy = jnp.concatenate([ym, ym], axis=1)

    def layer(i):
        if i < 0:
            return below()
        if i > 15:
            return above()
        return field(i)

    for i in rows:
        pos = domain * 16 + (i + 5)
        low = (i + 5) & -(i + 5)
        w = layer(i)
        if low <= 4:
            w = w - 0.5 * (layer(i - low) + layer(i + low))
        w = w * jnp.where(kept(pos, gx), 1.0, 0.0)
        high, rest = split2(w)
        u = jnp.dot(yy, jnp.concatenate([high, rest], axis=0), preferred_element_type=F32)
        high, rest = split2(u)
        v = jnp.dot(high, zm, preferred_element_type=F32)
        v = v + jnp.dot(rest, zm, preferred_element_type=F32)
        store(i, v.astype(BF16))


def early_kernel(gap_ref, field_ref, after_ref, all_ref, *outs):
    del after_ref

    def store(i, value):
        if outs:
            outs[(i - 2) // 4][(i - 2) % 4] = value
        all_ref[i - 2] = value

    hier_rows(range(2, 14), lambda i: field_ref[0, i].astype(F32), None, None, gap_ref, store)


def late_kernel(gap_ref, field_ref, one_ref, two_ref, out_ref):
    odd = (lax.axis_index("dom") % 2).astype(F32)
    even = 1.0 - odd

    def below():
        return one_ref[0].astype(F32) * odd + two_ref[0].astype(F32) * even

    def above():
        return one_ref[0].astype(F32) * even + two_ref[0].astype(F32) * odd

    def store(i, value):
        out_ref[PIECES[0].index(i)] = value

    hier_rows(PIECES[0], lambda i: field_ref[0, i].astype(F32), below, above, gap_ref, store)


def slots_kernel(owner_ref, dest_ref):
    group = lax.axis_index("grid")
    n = 256
    before = (
        lax.broadcasted_iota(jnp.int32, (n, n), 0) < lax.broadcasted_iota(jnp.int32, (n, n), 1)
    ).astype(BF16)
    ids = lax.broadcasted_iota(jnp.int32, (128, n), 0)
    count = jnp.zeros((128, 1), F32)
    for r in range(16):
        owner = jnp.concatenate([owner_ref[k : k + 1, :] for k in (2 * r, 2 * r + 1)], axis=1)
        hit = ids == owner
        one_hot = hit.astype(F32)
        earlier = jnp.dot(one_hot.astype(BF16), before, preferred_element_type=F32) + count
        slot = jnp.sum(one_hot * earlier, axis=0, keepdims=True).astype(jnp.int32)
        count = count + jnp.sum(one_hot, axis=1, keepdims=True)
        apart = (owner >> 5) ^ (group >> 1)
        row = (apart * 16 + (owner & 15)) * 64 + slot
        row = jnp.where(((owner >> 4) & 1) == (group & 1), row, 4096)
        dest_ref[2 * r : 2 * r + 1, :] = row[:, 0:128]
        dest_ref[2 * r + 1 : 2 * r + 2, :] = row[:, 128:256]


def place_kernel(dest_ref, flag_ref, coef_ref, own_late, own_early, core_late, core_early, *refs):
    outs = refs[0:4]
    low_ref, high_ref, packed = refs[4:7]
    group = lax.axis_index("grid")
    w0 = (coef_ref[group] * (1 - flag_ref[group])).astype(F32)
    w1 = (coef_ref[group ^ 1] * (1 - flag_ref[group ^ 1])).astype(F32)

    def add(i, own, core):
        p = w0 * own.astype(F32) + w1 * core.astype(F32)
        low_ref[pl.ds(i * 128, 128), :] = p[:, 0:128]
        high_ref[pl.ds(i * 128, 128), :] = p[:, 128:256]

    for j, i in enumerate(PIECES[0]):
        add(i, own_late[j], core_late[j])
    for i in range(2, 14):
        add(i, own_early[i - 2], core_early[i - 2])
    packed[...] = jnp.zeros_like(packed)

    def step(t, carry):
        base = pl.multiple_of(t * 64, 64)
        for u in range(64):
            packed[pl.ds(dest_ref[2 * base + 2 * u], 1), :] = low_ref[pl.ds(base + u, 1), :]
            packed[pl.ds(dest_ref[2 * base + 2 * u + 1], 1), :] = high_ref[pl.ds(base + u, 1), :]
        return carry

    lax.fori_loop(0, 32, step, 0)
    for q in range(4):
        outs[q][...] = packed[pl.ds(q * 1024, 1024), :].astype(BF16).reshape(16, 64, 128)


def reach(gap_ref, group, other):
    gx, gy = (jnp.maximum(gap_ref[k, group], gap_ref[k, other]) for k in (0, 1))
    rx = jnp.minimum(gx, 2)
    ry = jnp.minimum(gy, 2 - rx)
    return rx, ry, 2 - rx - ry


def picks(length, full_dim, part, skip):
    pos = lax.broadcasted_iota(jnp.int32, (length, length), full_dim) + 1
    place = lax.broadcasted_iota(jnp.int32, (length, length), 1 - full_dim) + 1
    hit = place == part * (length >> skip) + (pos >> skip)
    return jnp.where(hit & kept(pos, skip), 1.0, 0.0).astype(BF16)


def cases(gap_ref, group, other, work):
    rx, ry, _ = reach(gap_ref, group, other)
    for cx in range(3):
        for cy in range(3 - cx):

            @pl.when((rx == cx) & (ry == cy))
            def _():
                work(cx, cy, 2 - cx - cy)


def pack_kernel(gap_ref, partner_ref, late_ref, early_ref, near_ref, far_ref):
    group = lax.axis_index("grid")

    def row(i):
        return early_ref[i - 2] if 2 <= i < 14 else late_ref[PIECES[0].index(i)]

    for m, out_ref in ((1, near_ref), (2, far_ref)):
        target = group ^ (2 * m)

        def work(rx, ry, rz):
            across = [picks(256, 0, part, rz) for part in range(1 << rz)]
            down = [picks(128, 1, part, ry) for part in range(1 << ry)]
            for slab in range(4):
                runs = []
                for y in range(1 << ry):
                    first = (slab << (2 - rx)) + y
                    rows = [row(((first + (z << ry) + 1) << rx) - 1) for z in range(1 << rz)]
                    if rz:
                        hits = [jnp.dot(r, a, preferred_element_type=F32) for r, a in zip(rows, across)]
                        runs.append(sum(hits[1:], hits[0]).astype(BF16))
                    else:
                        runs.append(rows[0])
                if ry:
                    hits = [jnp.dot(d, r, preferred_element_type=F32) for d, r in zip(down, runs)]
                    out_ref[slab] = sum(hits[1:], hits[0]).astype(BF16)
                else:
                    out_ref[slab] = runs[0]

        @pl.when(partner_ref[target] == group)
        def _():
            cases(gap_ref, group, target, work)

        @pl.when(partner_ref[target] != group)
        def _():
            out_ref[...] = jnp.zeros_like(out_ref)


def diff_kernel(gap_ref, partner_ref, own_late, own_early, core_late, core_early, *refs):
    near_ref, far_ref, out_ref, came_ref = refs
    group = lax.axis_index("grid")
    domain = lax.axis_index("dom")
    other = partner_ref[group]
    gx, gy, gz = (jnp.maximum(gap_ref[k, group], gap_ref[k, other]) for k in range(3))
    dims = (128, 256)
    keep_y = kept(lax.broadcasted_iota(jnp.int32, dims, 0) + 1, gy)
    keep_z = kept(lax.broadcasted_iota(jnp.int32, dims, 1) + 1, gz)
    keep = jnp.where(keep_y & keep_z, 1.0, 0.0)
    flip = (other ^ group) >> 1

    def here(i):
        return jnp.where(kept(domain * 16 + (i + 5), gx), 1.0, 0.0)

    def own(i):
        return own_early[i - 2] if 2 <= i < 14 else own_late[PIECES[0].index(i)]

    def core(i):
        return core_early[i - 2] if 2 <= i < 14 else core_late[PIECES[0].index(i)]

    def work(rx, ry, rz):
        across = [picks(256, 1, part, rz) for part in range(1 << rz)]
        down = [picks(128, 0, part, ry) for part in range(1 << ry)]
        for i in range(16):
            if (i + 1) % (1 << rx):
                out_ref[0, i] = jnp.zeros(dims, F32)
                continue
            n = ((i + 1) >> rx) - 1
            sub = n % (1 << (2 - rx))
            theirs = came_ref[n >> (2 - rx)]
            if ry:
                theirs = jnp.dot(down[sub % (1 << ry)], theirs, preferred_element_type=F32)
            if rz:
                theirs = jnp.dot(theirs.astype(BF16), across[sub >> ry], preferred_element_type=F32)
            out_ref[0, i] = (keep * here(i)) * (own(i).astype(F32) - theirs.astype(F32))

    @pl.when(flip == 0)
    def _():
        for i in range(16):
            out_ref[0, i] = (keep * here(i)) * (own(i).astype(F32) - core(i).astype(F32))

    for kind, ref in ((1, near_ref), (2, far_ref)):

        @pl.when(flip == kind)
        def _():
            came_ref[...] = ref[...]

    @pl.when(flip != 0)
    def _():
        cases(gap_ref, group, other, work)


def route_kernel(partner_ref, r0, r1, r2, r3, m1, m2, m3):
    group = lax.axis_index("grid")
    held = (r0, r1, r2, r3)
    for m, out in ((1, m1), (2, m2), (3, m3)):
        target = group ^ (2 * m)
        far = ((partner_ref[target] ^ target) >> 1) == 2

        @pl.when(far)
        def _():
            out[...] = held[m ^ 2][...]

        @pl.when(jnp.logical_not(far))
        def _():
            out[...] = held[m ^ 1][...]


def relayed_diff_kernel(gap_ref, partner_ref, own_late, own_early, core_late, core_early, *refs):
    near, far = refs[0:4], refs[4:8]
    out_ref = refs[8]
    group = lax.axis_index("grid")
    domain = lax.axis_index("dom")
    other = partner_ref[group]
    gx, gy, gz = (jnp.maximum(gap_ref[k, group], gap_ref[k, other]) for k in range(3))
    dims = (128, 256)
    keep_y = kept(lax.broadcasted_iota(jnp.int32, dims, 0) + 1, gy)
    keep_z = kept(lax.broadcasted_iota(jnp.int32, dims, 1) + 1, gz)
    keep = jnp.where(keep_y & keep_z, 1.0, 0.0)
    flip = (other ^ group) >> 1

    def write(theirs):
        for q in range(4):
            for j, i in enumerate(PIECES[q]):
                own = own_early[i - 2] if q else own_late[j]
                here = keep * jnp.where(kept(domain * 16 + (i + 5), gx), 1.0, 0.0)
                out_ref[0, i] = here * (own.astype(F32) - theirs(q, j, i).astype(F32))

    @pl.when(flip == 0)
    def _():
        write(lambda q, j, i: core_early[i - 2] if q else core_late[j])

    @pl.when(flip == 1)
    def _():
        write(lambda q, j, i: near[q][j])

    @pl.when(flip == 2)
    def _():
        write(lambda q, j, i: far[q][j])


def fits_kernel(gap_ref, partner_ref, fits_ref):
    fits = jnp.int32(1)
    for group in range(8):
        other = partner_ref[group]
        skips = jnp.int32(0)
        for k in range(3):
            skips = skips + jnp.maximum(gap_ref[k, group], gap_ref[k, other])
        fits = jnp.where((other != (group ^ 1)) & (skips < 2), 0, fits)
    fits_ref[0] = fits


def sum_kernel(p0, p1, p2, p3, out_ref):
    total = (p0[...].astype(F32) + p1[...].astype(F32)) + (p2[...].astype(F32) + p3[...].astype(F32))
    for rank, k in enumerate(ORDER):
        out_ref[rank] = total[k].astype(BF16)


def owned_kernel(came_ref, out_ref):
    for rank, k in enumerate(ORDER):
        out_ref[0, k] = came_ref[rank].astype(F32)


def call(kernel, outs, ins, scratch=(), flops=0, nbytes=1 << 20, name=None):
    many = isinstance(outs, (list, tuple))
    return pl.pallas_call(
        kernel,
        out_shape=outs,
        in_specs=ins,
        out_specs=[vmem() for _ in outs] if many else vmem(),
        scratch_shapes=scratch,
        compiler_params=params(),
        cost_estimate=cost(flops, nbytes),
        name=name,
    )


def flipped(value, axis, bits):
    return lax.ppermute(value, axis, [(i, i ^ bits) for i in range(lax.axis_size(axis))])


def program(small, nodal, gaps, partner, flags, coefs, owners):
    odd = lax.axis_index("dom") % 2

    first = lax.dynamic_index_in_dim(nodal[0], 15 - 12 * odd, 0)
    second = lax.dynamic_index_in_dim(nodal[0], 3 + 12 * odd, 0)
    one = flipped(first, "dom", 1)
    two = lax.ppermute(
        second, "dom", [(i, i + 1) for i in range(1, 15, 2)] + [(i + 1, i) for i in range(1, 15, 2)]
    )

    piece = shape((4, 128, 256), BF16)
    inner = shape((12, 128, 256), BF16)
    early, *pieces = call(
        early_kernel, [inner] + [piece] * (0 if small else 3), [smem(), vmem(), anywhere()],
        flops=10**9, nbytes=2 << 20, name="early",
    )(gaps, nodal, second)
    early, one, two = lax.optimization_barrier((early, one, two))
    core_early = flipped(early, "grid", 1)
    dest = call(slots_kernel, shape((32, 128), jnp.int32), [vmem()], flops=10**9, name="slots")(
        owners.reshape(32, 128)
    ).reshape(4096)
    late = call(late_kernel, piece, [smem()] + [vmem()] * 3,
                flops=10**9, name="late")(gaps, nodal, one, two)
    core_late = flipped(late, "grid", 1)
    held = (late, early, core_late, core_early)

    bundle = shape((16, 64, 128), BF16)
    packed = call(
        place_kernel, [bundle] * 4, [smem()] * 3 + [vmem()] * 4,
        scratch=[pltpu.VMEM((2048, 128), F32), pltpu.VMEM((2048, 128), F32), pltpu.VMEM((4104, 128), F32)],
        flops=10**7, nbytes=16 << 20, name="place",
    )(dest, flags, coefs, *held)
    summed = [packed[0]] + [flipped(packed[b], "grid", 2 * b) for b in (1, 2, 3)]

    if small:
        near, far = call(
            pack_kernel, [piece] * 2, [smem(), smem(), vmem(), vmem()],
            flops=10**9, nbytes=2 << 20, name="pack",
        )(gaps, partner, late, early)
        theirs = (flipped(near, "grid", 2), flipped(far, "grid", 4))
    else:
        got = [late] + [flipped(pieces[b - 1], "grid", 2 * b) for b in (1, 2, 3)]
        sent = call(route_kernel, [piece] * 3, [smem()] + [vmem()] * 4, name="route")(partner, *got)
        came = [None] + [flipped(sent[m - 1], "grid", 2 * m) for m in (1, 2, 3)]
        theirs = (came[1], got[1], came[3], came[2], came[2], came[3], got[2], came[1])

    total = call(sum_kernel, bundle, [vmem()] * 4, name="sum")(*summed)
    moved = lax.all_to_all(total, "dom", 0, 0, tiled=True, axis_index_groups=[ORDER])
    owned = call(owned_kernel, shape((1, 16, 64, 128), F32), [vmem()], name="owned")(moved)

    diff = call(
        diff_kernel if small else relayed_diff_kernel, shape((1, 16, 128, 256), F32),
        [smem()] * 2 + [vmem()] * (4 + len(theirs)),
        scratch=[pltpu.VMEM((4, 128, 256), BF16)] if small else (), nbytes=6 << 20, name="diff",
    )(gaps, partner, *held, *theirs)
    return diff, owned


def body(nodal, level_gap, partner, flags, coefs, owners):
    gaps = level_gap.T
    fits = pl.pallas_call(
        fits_kernel,
        out_shape=shape((1,), jnp.int32),
        in_specs=[smem(), smem()],
        out_specs=smem(),
        name="fits",
    )(gaps, partner)
    return lax.cond(
        fits[0] != 0,
        functools.partial(program, True),
        functools.partial(program, False),
        nodal, gaps, partner, flags, coefs, owners,
    )


def solution(mesh):
    in_specs = (P("grid", "dom", None, None), P(), P(), P(), P(), P("dom", None))
    out_specs = (P("grid", "dom", None, None), P(("grid", "dom"), None, None, None))
    return jax.shard_map(body, mesh=mesh, in_specs=in_specs, out_specs=out_specs, check_vma=False)
```

```python
import functools

import jax
import jax.numpy as jnp
from jax import lax
from jax.experimental import pallas as pl
from jax.experimental.pallas import tpu as pltpu
from jax.sharding import PartitionSpec as P

F32 = jnp.float32
BF16 = jnp.bfloat16
ORDER = [15, 14, 13, 12, 11, 10, 9, 8, 7, 6, 5, 4, 3, 2, 1, 0]
PIECES = ((14, 15, 0, 1), (2, 3, 4, 5), (6, 7, 8, 9), (10, 11, 12, 13))


def hier_matrix(length, out_dim, gap):
    pos = lax.broadcasted_iota(jnp.int32, (length, length), out_dim) + 1
    source = lax.broadcasted_iota(jnp.int32, (length, length), 1 - out_dim) + 1
    low = pos & -pos
    away = jnp.abs(source - pos)
    value = jnp.where(away == 0, 1.0, jnp.where(away == low, -0.5, 0.0))
    return jnp.where(kept(pos, gap), value, 0.0).astype(BF16)


def vmem():
    return pl.BlockSpec(memory_space=pltpu.VMEM)


def smem():
    return pl.BlockSpec(memory_space=pltpu.SMEM)


def anywhere():
    return pl.BlockSpec(memory_space=pltpu.HBM)


def shape(dims, dtype):
    return jax.ShapeDtypeStruct(dims, dtype)


def params():
    return pltpu.CompilerParams(vmem_limit_bytes=8 * 1024 * 1024)


def cost(flops, nbytes):
    return pl.CostEstimate(flops=flops, bytes_accessed=nbytes, transcendentals=0)


def kept(iota_pos, gap):
    return (iota_pos & ((1 << gap) - 1)) == 0


def split2(w):
    high = w.astype(BF16)
    return high, (w - high.astype(F32)).astype(BF16)


def hier_rows(rows, field, below, above, gap_ref, store):
    group = lax.axis_index("grid")
    domain = lax.axis_index("dom")
    gx, gy, gz = gap_ref[0, group], gap_ref[1, group], gap_ref[2, group]
    ym = hier_matrix(128, 0, gy)
    zm = hier_matrix(256, 1, gz)
    yy = jnp.concatenate([ym, ym], axis=1)

    def layer(i):
        if i < 0:
            return below()
        if i > 15:
            return above()
        return field(i)

    for i in rows:
        pos = domain * 16 + (i + 5)
        low = (i + 5) & -(i + 5)
        w = layer(i)
        if low <= 4:
            w = w - 0.5 * (layer(i - low) + layer(i + low))
        w = w * jnp.where(kept(pos, gx), 1.0, 0.0)
        high, rest = split2(w)
        u = jnp.dot(yy, jnp.concatenate([high, rest], axis=0), preferred_element_type=F32)
        high, rest = split2(u)
        v = jnp.dot(high, zm, preferred_element_type=F32)
        v = v + jnp.dot(rest, zm, preferred_element_type=F32)
        store(i, v.astype(BF16))


def early_kernel(gap_ref, field_ref, after_ref, all_ref, *outs):
    del after_ref

    def store(i, value):
        if outs:
            outs[(i - 2) // 4][(i - 2) % 4] = value
        all_ref[i - 2] = value

    hier_rows(range(2, 14), lambda i: field_ref[0, i].astype(F32), None, None, gap_ref, store)


def late_kernel(gap_ref, field_ref, one_ref, two_ref, out_ref):
    odd = (lax.axis_index("dom") % 2).astype(F32)
    even = 1.0 - odd

    def below():
        return one_ref[0].astype(F32) * odd + two_ref[0].astype(F32) * even

    def above():
        return one_ref[0].astype(F32) * even + two_ref[0].astype(F32) * odd

    def store(i, value):
        out_ref[PIECES[0].index(i)] = value

    hier_rows(PIECES[0], lambda i: field_ref[0, i].astype(F32), below, above, gap_ref, store)


def slots_kernel(owner_ref, dest_ref):
    group = lax.axis_index("grid")
    n = 256
    before = (
        lax.broadcasted_iota(jnp.int32, (n, n), 0) < lax.broadcasted_iota(jnp.int32, (n, n), 1)
    ).astype(BF16)
    ids = lax.broadcasted_iota(jnp.int32, (128, n), 0)
    count = jnp.zeros((128, 1), F32)
    for r in range(16):
        owner = jnp.concatenate([owner_ref[k : k + 1, :] for k in (2 * r, 2 * r + 1)], axis=1)
        hit = ids == owner
        one_hot = hit.astype(F32)
        earlier = jnp.dot(one_hot.astype(BF16), before, preferred_element_type=F32) + count
        slot = jnp.sum(one_hot * earlier, axis=0, keepdims=True).astype(jnp.int32)
        count = count + jnp.sum(one_hot, axis=1, keepdims=True)
        apart = (owner >> 5) ^ (group >> 1)
        row = (apart * 16 + (owner & 15)) * 64 + slot
        row = jnp.where(((owner >> 4) & 1) == (group & 1), row, 4096)
        dest_ref[2 * r : 2 * r + 1, :] = row[:, 0:128]
        dest_ref[2 * r + 1 : 2 * r + 2, :] = row[:, 128:256]


def place_kernel(dest_ref, flag_ref, coef_ref, own_late, own_early, core_late, core_early, *refs):
    outs = refs[0:4]
    low_ref, high_ref, packed = refs[4:7]
    group = lax.axis_index("grid")
    w0 = (coef_ref[group] * (1 - flag_ref[group])).astype(F32)
    w1 = (coef_ref[group ^ 1] * (1 - flag_ref[group ^ 1])).astype(F32)

    def add(i, own, core):
        p = w0 * own.astype(F32) + w1 * core.astype(F32)
        low_ref[pl.ds(i * 128, 128), :] = p[:, 0:128]
        high_ref[pl.ds(i * 128, 128), :] = p[:, 128:256]

    for j, i in enumerate(PIECES[0]):
        add(i, own_late[j], core_late[j])
    for i in range(2, 14):
        add(i, own_early[i - 2], core_early[i - 2])
    packed[...] = jnp.zeros_like(packed)

    def step(t, carry):
        base = pl.multiple_of(t * 64, 64)
        for u in range(64):
            packed[pl.ds(dest_ref[2 * base + 2 * u], 1), :] = low_ref[pl.ds(base + u, 1), :]
            packed[pl.ds(dest_ref[2 * base + 2 * u + 1], 1), :] = high_ref[pl.ds(base + u, 1), :]
        return carry

    lax.fori_loop(0, 32, step, 0)
    for q in range(4):
        outs[q][...] = packed[pl.ds(q * 1024, 1024), :].astype(BF16).reshape(16, 64, 128)


def reach(gap_ref, group, other):
    gx, gy = (jnp.maximum(gap_ref[k, group], gap_ref[k, other]) for k in (0, 1))
    rx = jnp.minimum(gx, 2)
    ry = jnp.minimum(gy, 2 - rx)
    return rx, ry, 2 - rx - ry


def picks(length, full_dim, part, skip):
    pos = lax.broadcasted_iota(jnp.int32, (length, length), full_dim) + 1
    place = lax.broadcasted_iota(jnp.int32, (length, length), 1 - full_dim) + 1
    hit = place == part * (length >> skip) + (pos >> skip)
    return jnp.where(hit & kept(pos, skip), 1.0, 0.0).astype(BF16)


def cases(gap_ref, group, other, work):
    rx, ry, _ = reach(gap_ref, group, other)
    for cx in range(3):
        for cy in range(3 - cx):

            @pl.when((rx == cx) & (ry == cy))
            def _():
                work(cx, cy, 2 - cx - cy)


def pack_kernel(gap_ref, partner_ref, late_ref, early_ref, near_ref, far_ref):
    group = lax.axis_index("grid")

    def row(i):
        return early_ref[i - 2] if 2 <= i < 14 else late_ref[PIECES[0].index(i)]

    for m, out_ref in ((1, near_ref), (2, far_ref)):
        target = group ^ (2 * m)

        def work(rx, ry, rz):
            across = [picks(256, 0, part, rz) for part in range(1 << rz)]
            down = [picks(128, 1, part, ry) for part in range(1 << ry)]
            for slab in range(4):
                runs = []
                for y in range(1 << ry):
                    first = (slab << (2 - rx)) + y
                    rows = [row(((first + (z << ry) + 1) << rx) - 1) for z in range(1 << rz)]
                    if rz:
                        hits = [jnp.dot(r, a, preferred_element_type=F32) for r, a in zip(rows, across)]
                        runs.append(sum(hits[1:], hits[0]).astype(BF16))
                    else:
                        runs.append(rows[0])
                if ry:
                    hits = [jnp.dot(d, r, preferred_element_type=F32) for d, r in zip(down, runs)]
                    out_ref[slab] = sum(hits[1:], hits[0]).astype(BF16)
                else:
                    out_ref[slab] = runs[0]

        @pl.when(partner_ref[target] == group)
        def _():
            cases(gap_ref, group, target, work)

        @pl.when(partner_ref[target] != group)
        def _():
            out_ref[...] = jnp.zeros_like(out_ref)


def diff_kernel(gap_ref, partner_ref, own_late, own_early, core_late, core_early, *refs):
    near_ref, far_ref, out_ref, came_ref = refs
    group = lax.axis_index("grid")
    domain = lax.axis_index("dom")
    other = partner_ref[group]
    gx, gy, gz = (jnp.maximum(gap_ref[k, group], gap_ref[k, other]) for k in range(3))
    dims = (128, 256)
    keep_y = kept(lax.broadcasted_iota(jnp.int32, dims, 0) + 1, gy)
    keep_z = kept(lax.broadcasted_iota(jnp.int32, dims, 1) + 1, gz)
    keep = jnp.where(keep_y & keep_z, 1.0, 0.0)
    flip = (other ^ group) >> 1

    def here(i):
        return jnp.where(kept(domain * 16 + (i + 5), gx), 1.0, 0.0)

    def own(i):
        return own_early[i - 2] if 2 <= i < 14 else own_late[PIECES[0].index(i)]

    def core(i):
        return core_early[i - 2] if 2 <= i < 14 else core_late[PIECES[0].index(i)]

    def work(rx, ry, rz):
        across = [picks(256, 1, part, rz) for part in range(1 << rz)]
        down = [picks(128, 0, part, ry) for part in range(1 << ry)]
        for i in range(16):
            if (i + 1) % (1 << rx):
                out_ref[0, i] = jnp.zeros(dims, F32)
                continue
            n = ((i + 1) >> rx) - 1
            sub = n % (1 << (2 - rx))
            theirs = came_ref[n >> (2 - rx)]
            if ry:
                theirs = jnp.dot(down[sub % (1 << ry)], theirs, preferred_element_type=F32)
            if rz:
                theirs = jnp.dot(theirs.astype(BF16), across[sub >> ry], preferred_element_type=F32)
            out_ref[0, i] = (keep * here(i)) * (own(i).astype(F32) - theirs.astype(F32))

    @pl.when(flip == 0)
    def _():
        for i in range(16):
            out_ref[0, i] = (keep * here(i)) * (own(i).astype(F32) - core(i).astype(F32))

    for kind, ref in ((1, near_ref), (2, far_ref)):

        @pl.when(flip == kind)
        def _():
            came_ref[...] = ref[...]

    @pl.when(flip != 0)
    def _():
        cases(gap_ref, group, other, work)


def route_kernel(partner_ref, r0, r1, r2, r3, m1, m2, m3):
    group = lax.axis_index("grid")
    held = (r0, r1, r2, r3)
    for m, out in ((1, m1), (2, m2), (3, m3)):
        target = group ^ (2 * m)
        far = ((partner_ref[target] ^ target) >> 1) == 2

        @pl.when(far)
        def _():
            out[...] = held[m ^ 2][...]

        @pl.when(jnp.logical_not(far))
        def _():
            out[...] = held[m ^ 1][...]


def relayed_diff_kernel(gap_ref, partner_ref, own_late, own_early, core_late, core_early, *refs):
    near, far = refs[0:4], refs[4:8]
    out_ref = refs[8]
    group = lax.axis_index("grid")
    domain = lax.axis_index("dom")
    other = partner_ref[group]
    gx, gy, gz = (jnp.maximum(gap_ref[k, group], gap_ref[k, other]) for k in range(3))
    dims = (128, 256)
    keep_y = kept(lax.broadcasted_iota(jnp.int32, dims, 0) + 1, gy)
    keep_z = kept(lax.broadcasted_iota(jnp.int32, dims, 1) + 1, gz)
    keep = jnp.where(keep_y & keep_z, 1.0, 0.0)
    flip = (other ^ group) >> 1

    def write(theirs):
        for q in range(4):
            for j, i in enumerate(PIECES[q]):
                own = own_early[i - 2] if q else own_late[j]
                here = keep * jnp.where(kept(domain * 16 + (i + 5), gx), 1.0, 0.0)
                out_ref[0, i] = here * (own.astype(F32) - theirs(q, j, i).astype(F32))

    @pl.when(flip == 0)
    def _():
        write(lambda q, j, i: core_early[i - 2] if q else core_late[j])

    @pl.when(flip == 1)
    def _():
        write(lambda q, j, i: near[q][j])

    @pl.when(flip == 2)
    def _():
        write(lambda q, j, i: far[q][j])


def head_kernel(field_hbm, gap_hbm, partner_hbm, fits_ref, first_hbm, second_hbm, gap_ref, partner_ref, sems):
    odd = lax.axis_index("dom") % 2
    copies = [
        pltpu.make_async_copy(gap_hbm, gap_ref, sems.at[0]),
        pltpu.make_async_copy(partner_hbm, partner_ref, sems.at[1]),
        pltpu.make_async_copy(field_hbm.at[0, 15 - 12 * odd], first_hbm.at[0], sems.at[2]),
        pltpu.make_async_copy(field_hbm.at[0, 3 + 12 * odd], second_hbm.at[0], sems.at[3]),
    ]
    for copy in copies:
        copy.start()
    for copy in copies[:2]:
        copy.wait()
    fits = jnp.int32(1)
    for group in range(8):
        other = partner_ref[group]
        skips = jnp.int32(0)
        for k in range(3):
            skips = skips + jnp.maximum(gap_ref[k, group], gap_ref[k, other])
        fits = jnp.where((other != (group ^ 1)) & (skips < 2), 0, fits)
    fits_ref[0] = fits
    for copy in copies[2:]:
        copy.wait()


def sum_kernel(p0, p1, p2, p3, out_ref):
    total = (p0[...].astype(F32) + p1[...].astype(F32)) + (p2[...].astype(F32) + p3[...].astype(F32))
    for rank, k in enumerate(ORDER):
        out_ref[rank] = total[k].astype(BF16)


def owned_kernel(came_ref, out_ref):
    for rank, k in enumerate(ORDER):
        out_ref[0, k] = came_ref[rank].astype(F32)


def call(kernel, outs, ins, scratch=(), flops=0, nbytes=1 << 20, name=None):
    many = isinstance(outs, (list, tuple))
    return pl.pallas_call(
        kernel,
        out_shape=outs,
        in_specs=ins,
        out_specs=[vmem() for _ in outs] if many else vmem(),
        scratch_shapes=scratch,
        compiler_params=params(),
        cost_estimate=cost(flops, nbytes),
        name=name,
    )


def flipped(value, axis, bits):
    return lax.ppermute(value, axis, [(i, i ^ bits) for i in range(lax.axis_size(axis))])


def program(small, first, second, nodal, gaps, partner, flags, coefs, owners):
    one = flipped(first, "dom", 1)
    two = lax.ppermute(
        second, "dom", [(i, i + 1) for i in range(1, 15, 2)] + [(i + 1, i) for i in range(1, 15, 2)]
    )

    piece = shape((4, 128, 256), BF16)
    inner = shape((12, 128, 256), BF16)
    early, *pieces = call(
        early_kernel, [inner] + [piece] * (0 if small else 3), [smem(), vmem(), anywhere()],
        flops=10**9, nbytes=2 << 20, name="early",
    )(gaps, nodal, second)
    early, one, two = lax.optimization_barrier((early, one, two))
    core_early = flipped(early, "grid", 1)
    dest = call(slots_kernel, shape((32, 128), jnp.int32), [vmem()], flops=10**9, name="slots")(
        owners.reshape(32, 128)
    ).reshape(4096)
    late = call(late_kernel, piece, [smem()] + [vmem()] * 3,
                flops=10**9, name="late")(gaps, nodal, one, two)
    core_late = flipped(late, "grid", 1)
    held = (late, early, core_late, core_early)

    bundle = shape((16, 64, 128), BF16)
    packed = call(
        place_kernel, [bundle] * 4, [smem()] * 3 + [vmem()] * 4,
        scratch=[pltpu.VMEM((2048, 128), F32), pltpu.VMEM((2048, 128), F32), pltpu.VMEM((4104, 128), F32)],
        flops=10**7, nbytes=16 << 20, name="place",
    )(dest, flags, coefs, *held)
    summed = [packed[0]] + [flipped(packed[b], "grid", 2 * b) for b in (2, 1, 3)]

    if small:
        near, far = call(
            pack_kernel, [piece] * 2, [smem(), smem(), vmem(), vmem()],
            flops=10**9, nbytes=2 << 20, name="pack",
        )(gaps, partner, late, early)
        theirs = (flipped(near, "grid", 2), flipped(far, "grid", 4))
    else:
        got = [late] + [flipped(pieces[b - 1], "grid", 2 * b) for b in (1, 2, 3)]
        sent = call(route_kernel, [piece] * 3, [smem()] + [vmem()] * 4, name="route")(partner, *got)
        came = [None] + [flipped(sent[m - 1], "grid", 2 * m) for m in (1, 2, 3)]
        theirs = (came[1], got[1], came[3], came[2], came[2], came[3], got[2], came[1])

    total = call(sum_kernel, bundle, [vmem()] * 4, name="sum")(*summed)
    moved = lax.all_to_all(total, "dom", 0, 0, tiled=True, axis_index_groups=[ORDER])
    owned = call(owned_kernel, shape((1, 16, 64, 128), F32), [vmem()], name="owned")(moved)

    diff = call(
        diff_kernel if small else relayed_diff_kernel, shape((1, 16, 128, 256), F32),
        [smem()] * 2 + [vmem()] * (4 + len(theirs)),
        scratch=[pltpu.VMEM((4, 128, 256), BF16)] if small else (), nbytes=6 << 20, name="diff",
    )(gaps, partner, *held, *theirs)
    return diff, owned


def body(nodal, level_gap, partner, flags, coefs, owners):
    gaps = level_gap.T
    edge = shape((1, 128, 256), BF16)
    fits, first, second = pl.pallas_call(
        head_kernel,
        out_shape=[shape((1,), jnp.int32), edge, edge],
        in_specs=[anywhere()] * 3,
        out_specs=[smem(), anywhere(), anywhere()],
        scratch_shapes=[
            pltpu.SMEM((3, 8), jnp.int32), pltpu.SMEM((8,), jnp.int32), pltpu.SemaphoreType.DMA((4,))
        ],
        compiler_params=pltpu.CompilerParams(vmem_limit_bytes=8 * 1024 * 1024),
        name="head",
    )(nodal, gaps, partner)
    return lax.cond(
        fits[0] != 0,
        functools.partial(program, True),
        functools.partial(program, False),
        first, second, nodal, gaps, partner, flags, coefs, owners,
    )


def solution(mesh):
    in_specs = (P("grid", "dom", None, None), P(), P(), P(), P(), P("dom", None))
    out_specs = (P("grid", "dom", None, None), P(("grid", "dom"), None, None, None))
    return jax.shard_map(body, mesh=mesh, in_specs=in_specs, out_specs=out_specs, check_vma=False)
```

```python
import functools

import jax
import jax.numpy as jnp
from jax import lax
from jax.experimental import pallas as pl
from jax.experimental.pallas import tpu as pltpu
from jax.sharding import PartitionSpec as P

F32 = jnp.float32
BF16 = jnp.bfloat16
ORDER = [15, 14, 13, 12, 11, 10, 9, 8, 7, 6, 5, 4, 3, 2, 1, 0]
PIECES = ((14, 15, 0, 1), (2, 3, 4, 5), (6, 7, 8, 9), (10, 11, 12, 13))


def hier_matrix(length, out_dim, gap):
    pos = lax.broadcasted_iota(jnp.int32, (length, length), out_dim) + 1
    source = lax.broadcasted_iota(jnp.int32, (length, length), 1 - out_dim) + 1
    low = pos & -pos
    away = jnp.abs(source - pos)
    value = jnp.where(away == 0, 1.0, jnp.where(away == low, -0.5, 0.0))
    return jnp.where(kept(pos, gap), value, 0.0).astype(BF16)


def vmem():
    return pl.BlockSpec(memory_space=pltpu.VMEM)


def smem():
    return pl.BlockSpec(memory_space=pltpu.SMEM)


def anywhere():
    return pl.BlockSpec(memory_space=pltpu.HBM)


def shape(dims, dtype):
    return jax.ShapeDtypeStruct(dims, dtype)


def params():
    return pltpu.CompilerParams(vmem_limit_bytes=8 * 1024 * 1024)


def cost(flops, nbytes):
    return pl.CostEstimate(flops=flops, bytes_accessed=nbytes, transcendentals=0)


def kept(iota_pos, gap):
    return (iota_pos & ((1 << gap) - 1)) == 0


def split2(w):
    high = w.astype(BF16)
    return high, (w - high.astype(F32)).astype(BF16)


def hier_rows(rows, field, below, above, gap_ref, store):
    group = lax.axis_index("grid")
    domain = lax.axis_index("dom")
    gx, gy, gz = gap_ref[0, group], gap_ref[1, group], gap_ref[2, group]
    ym = hier_matrix(128, 0, gy)
    zm = hier_matrix(256, 1, gz)
    yy = jnp.concatenate([ym, ym], axis=1)

    def layer(i):
        if i < 0:
            return below()
        if i > 15:
            return above()
        return field(i)

    rows = list(rows)
    for first in range(0, len(rows), 4):
        group_rows = rows[first : first + 4]
        results = []
        for i in group_rows:
            pos = domain * 16 + (i + 5)
            low = (i + 5) & -(i + 5)
            w = layer(i)
            if low <= 4:
                w = w - 0.5 * (layer(i - low) + layer(i + low))
            w = w * jnp.where(kept(pos, gx), 1.0, 0.0)
            high, rest = split2(w)
            results.append(
                jnp.dot(yy, jnp.concatenate([high, rest], axis=0), preferred_element_type=F32)
            )
        high, rest = split2(jnp.concatenate(results, axis=0))
        v = jnp.dot(high, zm, preferred_element_type=F32)
        v = (v + jnp.dot(rest, zm, preferred_element_type=F32)).astype(BF16)
        for n, i in enumerate(group_rows):
            store(i, v[n * 128 : (n + 1) * 128])


def early_kernel(gap_ref, field_ref, after_ref, all_ref, *outs):
    del after_ref

    def store(i, value):
        if outs:
            outs[(i - 2) // 4][(i - 2) % 4] = value
        all_ref[i - 2] = value

    hier_rows(range(2, 14), lambda i: field_ref[0, i].astype(F32), None, None, gap_ref, store)


def late_kernel(gap_ref, field_ref, one_ref, two_ref, out_ref):
    odd = (lax.axis_index("dom") % 2).astype(F32)
    even = 1.0 - odd

    def below():
        return one_ref[0].astype(F32) * odd + two_ref[0].astype(F32) * even

    def above():
        return one_ref[0].astype(F32) * even + two_ref[0].astype(F32) * odd

    def store(i, value):
        out_ref[PIECES[0].index(i)] = value

    hier_rows(PIECES[0], lambda i: field_ref[0, i].astype(F32), below, above, gap_ref, store)


def slots_kernel(owner_ref, dest_ref):
    group = lax.axis_index("grid")
    n = 256
    before = (
        lax.broadcasted_iota(jnp.int32, (n, n), 0) < lax.broadcasted_iota(jnp.int32, (n, n), 1)
    ).astype(BF16)
    ids = lax.broadcasted_iota(jnp.int32, (128, n), 0)
    count = jnp.zeros((128, 1), F32)
    for r in range(16):
        owner = jnp.concatenate([owner_ref[k : k + 1, :] for k in (2 * r, 2 * r + 1)], axis=1)
        hit = ids == owner
        one_hot = hit.astype(F32)
        earlier = jnp.dot(one_hot.astype(BF16), before, preferred_element_type=F32) + count
        slot = jnp.sum(one_hot * earlier, axis=0, keepdims=True).astype(jnp.int32)
        count = count + jnp.sum(one_hot, axis=1, keepdims=True)
        apart = (owner >> 5) ^ (group >> 1)
        row = (apart * 16 + (owner & 15)) * 64 + slot
        row = jnp.where(((owner >> 4) & 1) == (group & 1), row, 4096)
        dest_ref[2 * r : 2 * r + 1, :] = row[:, 0:128]
        dest_ref[2 * r + 1 : 2 * r + 2, :] = row[:, 128:256]


def place_kernel(dest_ref, flag_ref, coef_ref, own_late, own_early, core_late, core_early, *refs):
    outs = refs[0:4]
    low_ref, high_ref, packed = refs[4:7]
    group = lax.axis_index("grid")
    w0 = (coef_ref[group] * (1 - flag_ref[group])).astype(F32)
    w1 = (coef_ref[group ^ 1] * (1 - flag_ref[group ^ 1])).astype(F32)

    def add(i, own, core):
        p = w0 * own.astype(F32) + w1 * core.astype(F32)
        low_ref[pl.ds(i * 128, 128), :] = p[:, 0:128]
        high_ref[pl.ds(i * 128, 128), :] = p[:, 128:256]

    for j, i in enumerate(PIECES[0]):
        add(i, own_late[j], core_late[j])
    for i in range(2, 14):
        add(i, own_early[i - 2], core_early[i - 2])
    packed[...] = jnp.zeros_like(packed)

    def step(t, carry):
        base = pl.multiple_of(t * 64, 64)
        for u in range(64):
            packed[pl.ds(dest_ref[2 * base + 2 * u], 1), :] = low_ref[pl.ds(base + u, 1), :]
            packed[pl.ds(dest_ref[2 * base + 2 * u + 1], 1), :] = high_ref[pl.ds(base + u, 1), :]
        return carry

    lax.fori_loop(0, 32, step, 0)
    for q in range(4):
        outs[q][...] = packed[pl.ds(q * 1024, 1024), :].astype(BF16).reshape(16, 64, 128)


def reach(gap_ref, group, other):
    gx, gy = (jnp.maximum(gap_ref[k, group], gap_ref[k, other]) for k in (0, 1))
    rx = jnp.minimum(gx, 2)
    ry = jnp.minimum(gy, 2 - rx)
    return rx, ry, 2 - rx - ry


def picks(length, full_dim, part, skip):
    pos = lax.broadcasted_iota(jnp.int32, (length, length), full_dim) + 1
    place = lax.broadcasted_iota(jnp.int32, (length, length), 1 - full_dim) + 1
    hit = place == part * (length >> skip) + (pos >> skip)
    return jnp.where(hit & kept(pos, skip), 1.0, 0.0).astype(BF16)


def cases(gap_ref, group, other, work):
    rx, ry, _ = reach(gap_ref, group, other)
    for cx in range(3):
        for cy in range(3 - cx):

            @pl.when((rx == cx) & (ry == cy))
            def _():
                work(cx, cy, 2 - cx - cy)


def pack_kernel(gap_ref, partner_ref, late_ref, early_ref, near_ref, far_ref):
    group = lax.axis_index("grid")

    def row(i):
        return early_ref[i - 2] if 2 <= i < 14 else late_ref[PIECES[0].index(i)]

    for m, out_ref in ((1, near_ref), (2, far_ref)):
        target = group ^ (2 * m)

        def work(rx, ry, rz):
            across = [picks(256, 0, part, rz) for part in range(1 << rz)]
            down = [picks(128, 1, part, ry) for part in range(1 << ry)]
            for slab in range(4):
                runs = []
                for y in range(1 << ry):
                    first = (slab << (2 - rx)) + y
                    rows = [row(((first + (z << ry) + 1) << rx) - 1) for z in range(1 << rz)]
                    if rz:
                        hits = [jnp.dot(r, a, preferred_element_type=F32) for r, a in zip(rows, across)]
                        runs.append(sum(hits[1:], hits[0]).astype(BF16))
                    else:
                        runs.append(rows[0])
                if ry:
                    hits = [jnp.dot(d, r, preferred_element_type=F32) for d, r in zip(down, runs)]
                    out_ref[slab] = sum(hits[1:], hits[0]).astype(BF16)
                else:
                    out_ref[slab] = runs[0]

        @pl.when(partner_ref[target] == group)
        def _():
            cases(gap_ref, group, target, work)

        @pl.when(partner_ref[target] != group)
        def _():
            out_ref[...] = jnp.zeros_like(out_ref)


def diff_kernel(gap_ref, partner_ref, own_late, own_early, core_late, core_early, *refs):
    near_ref, far_ref, out_ref, came_ref = refs
    group = lax.axis_index("grid")
    domain = lax.axis_index("dom")
    other = partner_ref[group]
    gx, gy, gz = (jnp.maximum(gap_ref[k, group], gap_ref[k, other]) for k in range(3))
    dims = (128, 256)
    keep_y = kept(lax.broadcasted_iota(jnp.int32, dims, 0) + 1, gy)
    keep_z = kept(lax.broadcasted_iota(jnp.int32, dims, 1) + 1, gz)
    keep = jnp.where(keep_y & keep_z, 1.0, 0.0)
    flip = (other ^ group) >> 1

    def here(i):
        return jnp.where(kept(domain * 16 + (i + 5), gx), 1.0, 0.0)

    def own(i):
        return own_early[i - 2] if 2 <= i < 14 else own_late[PIECES[0].index(i)]

    def core(i):
        return core_early[i - 2] if 2 <= i < 14 else core_late[PIECES[0].index(i)]

    def work(rx, ry, rz):
        across = [picks(256, 1, part, rz) for part in range(1 << rz)]
        down = [picks(128, 0, part, ry) for part in range(1 << ry)]
        for i in range(16):
            if (i + 1) % (1 << rx):
                out_ref[0, i] = jnp.zeros(dims, F32)
                continue
            n = ((i + 1) >> rx) - 1
            sub = n % (1 << (2 - rx))
            theirs = came_ref[n >> (2 - rx)]
            if ry:
                theirs = jnp.dot(down[sub % (1 << ry)], theirs, preferred_element_type=F32)
            if rz:
                theirs = jnp.dot(theirs.astype(BF16), across[sub >> ry], preferred_element_type=F32)
            out_ref[0, i] = (keep * here(i)) * (own(i).astype(F32) - theirs.astype(F32))

    @pl.when(flip == 0)
    def _():
        for i in range(16):
            out_ref[0, i] = (keep * here(i)) * (own(i).astype(F32) - core(i).astype(F32))

    for kind, ref in ((1, near_ref), (2, far_ref)):

        @pl.when(flip == kind)
        def _():
            came_ref[...] = ref[...]

    @pl.when(flip != 0)
    def _():
        cases(gap_ref, group, other, work)


def route_kernel(partner_ref, r0, r1, r2, r3, m1, m2, m3):
    group = lax.axis_index("grid")
    held = (r0, r1, r2, r3)
    for m, out in ((1, m1), (2, m2), (3, m3)):
        target = group ^ (2 * m)
        far = ((partner_ref[target] ^ target) >> 1) == 2

        @pl.when(far)
        def _():
            out[...] = held[m ^ 2][...]

        @pl.when(jnp.logical_not(far))
        def _():
            out[...] = held[m ^ 1][...]


def relayed_diff_kernel(gap_ref, partner_ref, own_late, own_early, core_late, core_early, *refs):
    near, far = refs[0:4], refs[4:8]
    out_ref = refs[8]
    group = lax.axis_index("grid")
    domain = lax.axis_index("dom")
    other = partner_ref[group]
    gx, gy, gz = (jnp.maximum(gap_ref[k, group], gap_ref[k, other]) for k in range(3))
    dims = (128, 256)
    keep_y = kept(lax.broadcasted_iota(jnp.int32, dims, 0) + 1, gy)
    keep_z = kept(lax.broadcasted_iota(jnp.int32, dims, 1) + 1, gz)
    keep = jnp.where(keep_y & keep_z, 1.0, 0.0)
    flip = (other ^ group) >> 1

    def write(theirs):
        for q in range(4):
            for j, i in enumerate(PIECES[q]):
                own = own_early[i - 2] if q else own_late[j]
                here = keep * jnp.where(kept(domain * 16 + (i + 5), gx), 1.0, 0.0)
                out_ref[0, i] = here * (own.astype(F32) - theirs(q, j, i).astype(F32))

    @pl.when(flip == 0)
    def _():
        write(lambda q, j, i: core_early[i - 2] if q else core_late[j])

    @pl.when(flip == 1)
    def _():
        write(lambda q, j, i: near[q][j])

    @pl.when(flip == 2)
    def _():
        write(lambda q, j, i: far[q][j])


def head_kernel(field_hbm, gap_hbm, partner_hbm, fits_ref, first_hbm, second_hbm, gap_ref, partner_ref, sems):
    odd = lax.axis_index("dom") % 2
    copies = [
        pltpu.make_async_copy(gap_hbm, gap_ref, sems.at[0]),
        pltpu.make_async_copy(partner_hbm, partner_ref, sems.at[1]),
        pltpu.make_async_copy(field_hbm.at[0, 15 - 12 * odd], first_hbm.at[0], sems.at[2]),
        pltpu.make_async_copy(field_hbm.at[0, 3 + 12 * odd], second_hbm.at[0], sems.at[3]),
    ]
    for copy in copies:
        copy.start()
    for copy in copies[:2]:
        copy.wait()
    fits = jnp.int32(1)
    for group in range(8):
        other = partner_ref[group]
        skips = jnp.int32(0)
        for k in range(3):
            skips = skips + jnp.maximum(gap_ref[k, group], gap_ref[k, other])
        fits = jnp.where((other != (group ^ 1)) & (skips < 2), 0, fits)
    fits_ref[0] = fits
    for copy in copies[2:]:
        copy.wait()


def sum_kernel(p0, p1, p2, p3, out_ref):
    total = (p0[...].astype(F32) + p1[...].astype(F32)) + (p2[...].astype(F32) + p3[...].astype(F32))
    for rank, k in enumerate(ORDER):
        out_ref[rank] = total[k].astype(BF16)


def owned_kernel(came_ref, out_ref):
    for rank, k in enumerate(ORDER):
        out_ref[0, k] = came_ref[rank].astype(F32)


def call(kernel, outs, ins, scratch=(), flops=0, nbytes=1 << 20, name=None):
    many = isinstance(outs, (list, tuple))
    return pl.pallas_call(
        kernel,
        out_shape=outs,
        in_specs=ins,
        out_specs=[vmem() for _ in outs] if many else vmem(),
        scratch_shapes=scratch,
        compiler_params=params(),
        cost_estimate=cost(flops, nbytes),
        name=name,
    )


def flipped(value, axis, bits):
    return lax.ppermute(value, axis, [(i, i ^ bits) for i in range(lax.axis_size(axis))])


def program(small, first, second, nodal, gaps, partner, flags, coefs, owners):
    one = flipped(first, "dom", 1)
    two = lax.ppermute(
        second, "dom", [(i, i + 1) for i in range(1, 15, 2)] + [(i + 1, i) for i in range(1, 15, 2)]
    )

    piece = shape((4, 128, 256), BF16)
    inner = shape((12, 128, 256), BF16)
    early, *pieces = call(
        early_kernel, [inner] + [piece] * (0 if small else 3), [smem(), vmem(), anywhere()],
        flops=10**9, nbytes=2 << 20, name="early",
    )(gaps, nodal, second)
    early, one, two = lax.optimization_barrier((early, one, two))
    core_early = flipped(early, "grid", 1)
    dest = call(slots_kernel, shape((32, 128), jnp.int32), [vmem()], flops=10**9, name="slots")(
        owners.reshape(32, 128)
    ).reshape(4096)
    late = call(late_kernel, piece, [smem()] + [vmem()] * 3,
                flops=10**9, name="late")(gaps, nodal, one, two)
    core_late = flipped(late, "grid", 1)
    held = (late, early, core_late, core_early)

    bundle = shape((16, 64, 128), BF16)
    packed = call(
        place_kernel, [bundle] * 4, [smem()] * 3 + [vmem()] * 4,
        scratch=[pltpu.VMEM((2048, 128), F32), pltpu.VMEM((2048, 128), F32), pltpu.VMEM((4104, 128), F32)],
        flops=10**7, nbytes=16 << 20, name="place",
    )(dest, flags, coefs, *held)
    summed = [packed[0]] + [flipped(packed[b], "grid", 2 * b) for b in (2, 1, 3)]

    if small:
        near, far = call(
            pack_kernel, [piece] * 2, [smem(), smem(), vmem(), vmem()],
            flops=10**9, nbytes=2 << 20, name="pack",
        )(gaps, partner, late, early)
        theirs = (flipped(near, "grid", 2), flipped(far, "grid", 4))
    else:
        got = [late] + [flipped(pieces[b - 1], "grid", 2 * b) for b in (1, 2, 3)]
        sent = call(route_kernel, [piece] * 3, [smem()] + [vmem()] * 4, name="route")(partner, *got)
        came = [None] + [flipped(sent[m - 1], "grid", 2 * m) for m in (1, 2, 3)]
        theirs = (came[1], got[1], came[3], came[2], came[2], came[3], got[2], came[1])

    total = call(sum_kernel, bundle, [vmem()] * 4, name="sum")(*summed)
    moved = lax.all_to_all(total, "dom", 0, 0, tiled=True, axis_index_groups=[ORDER])
    owned = call(owned_kernel, shape((1, 16, 64, 128), F32), [vmem()], name="owned")(moved)

    diff = call(
        diff_kernel if small else relayed_diff_kernel, shape((1, 16, 128, 256), F32),
        [smem()] * 2 + [vmem()] * (4 + len(theirs)),
        scratch=[pltpu.VMEM((4, 128, 256), BF16)] if small else (), nbytes=6 << 20, name="diff",
    )(gaps, partner, *held, *theirs)
    return diff, owned


def body(nodal, level_gap, partner, flags, coefs, owners):
    gaps = level_gap.T
    edge = shape((1, 128, 256), BF16)
    fits, first, second = pl.pallas_call(
        head_kernel,
        out_shape=[shape((1,), jnp.int32), edge, edge],
        in_specs=[anywhere()] * 3,
        out_specs=[smem(), anywhere(), anywhere()],
        scratch_shapes=[
            pltpu.SMEM((3, 8), jnp.int32), pltpu.SMEM((8,), jnp.int32), pltpu.SemaphoreType.DMA((4,))
        ],
        compiler_params=pltpu.CompilerParams(vmem_limit_bytes=8 * 1024 * 1024),
        name="head",
    )(nodal, gaps, partner)
    return lax.cond(
        fits[0] != 0,
        functools.partial(program, True),
        functools.partial(program, False),
        first, second, nodal, gaps, partner, flags, coefs, owners,
    )


def solution(mesh):
    in_specs = (P("grid", "dom", None, None), P(), P(), P(), P(), P("dom", None))
    out_specs = (P("grid", "dom", None, None), P(("grid", "dom"), None, None, None))
    return jax.shard_map(body, mesh=mesh, in_specs=in_specs, out_specs=out_specs, check_vma=False)
```

```python
import functools

import jax
import jax.numpy as jnp
from jax import lax
from jax.experimental import pallas as pl
from jax.experimental.pallas import tpu as pltpu
from jax.sharding import PartitionSpec as P

F32 = jnp.float32
BF16 = jnp.bfloat16
ORDER = [15, 14, 13, 12, 11, 10, 9, 8, 7, 6, 5, 4, 3, 2, 1, 0]
PIECES = ((14, 15, 0, 1), (2, 3, 4, 5), (6, 7, 8, 9), (10, 11, 12, 13))


def hier_matrix(length, out_dim, gap):
    pos = lax.broadcasted_iota(jnp.int32, (length, length), out_dim) + 1
    source = lax.broadcasted_iota(jnp.int32, (length, length), 1 - out_dim) + 1
    low = pos & -pos
    away = jnp.abs(source - pos)
    value = jnp.where(away == 0, 1.0, jnp.where(away == low, -0.5, 0.0))
    return jnp.where(kept(pos, gap), value, 0.0).astype(BF16)


def vmem():
    return pl.BlockSpec(memory_space=pltpu.VMEM)


def smem():
    return pl.BlockSpec(memory_space=pltpu.SMEM)


def anywhere():
    return pl.BlockSpec(memory_space=pltpu.HBM)


def shape(dims, dtype):
    return jax.ShapeDtypeStruct(dims, dtype)


def params():
    return pltpu.CompilerParams(vmem_limit_bytes=8 * 1024 * 1024)


def cost(flops, nbytes):
    return pl.CostEstimate(flops=flops, bytes_accessed=nbytes, transcendentals=0)


def kept(iota_pos, gap):
    return (iota_pos & ((1 << gap) - 1)) == 0


def split2(w):
    high = w.astype(BF16)
    return high, (w - high.astype(F32)).astype(BF16)


def hier_rows(rows, field, below, above, gap_ref, store):
    group = lax.axis_index("grid")
    domain = lax.axis_index("dom")
    gx, gy, gz = gap_ref[0, group], gap_ref[1, group], gap_ref[2, group]
    ym = hier_matrix(128, 0, gy)
    zm = hier_matrix(256, 1, gz)
    yy = jnp.concatenate([ym, ym], axis=1)

    def layer(i):
        if i < 0:
            return below()
        if i > 15:
            return above()
        return field(i)

    rows = list(rows)
    for first in range(0, len(rows), 4):
        group_rows = rows[first : first + 4]
        results = []
        for i in group_rows:
            pos = domain * 16 + (i + 5)
            low = (i + 5) & -(i + 5)
            w = layer(i)
            if low <= 4:
                w = w - 0.5 * (layer(i - low) + layer(i + low))
            w = w * jnp.where(kept(pos, gx), 1.0, 0.0)
            high, rest = split2(w)
            results.append(
                jnp.dot(yy, jnp.concatenate([high, rest], axis=0), preferred_element_type=F32)
            )
        high, rest = split2(jnp.concatenate(results, axis=0))
        v = jnp.dot(high, zm, preferred_element_type=F32)
        v = (v + jnp.dot(rest, zm, preferred_element_type=F32)).astype(BF16)
        for n, i in enumerate(group_rows):
            store(i, v[n * 128 : (n + 1) * 128])


def early_kernel(gap_ref, field_ref, after_ref, all_ref, *outs):
    del after_ref

    def store(i, value):
        if outs:
            outs[(i - 2) // 4][(i - 2) % 4] = value
        all_ref[i - 2] = value

    hier_rows(range(2, 14), lambda i: field_ref[0, i].astype(F32), None, None, gap_ref, store)


def late_kernel(gap_ref, field_ref, one_ref, two_ref, out_ref):
    odd = (lax.axis_index("dom") % 2).astype(F32)
    even = 1.0 - odd

    def below():
        return one_ref[0].astype(F32) * odd + two_ref[0].astype(F32) * even

    def above():
        return one_ref[0].astype(F32) * even + two_ref[0].astype(F32) * odd

    def store(i, value):
        out_ref[PIECES[0].index(i)] = value

    hier_rows(PIECES[0], lambda i: field_ref[0, i].astype(F32), below, above, gap_ref, store)


def slots_kernel(owner_ref, dest_ref):
    group = lax.axis_index("grid")
    n = 256
    before = (
        lax.broadcasted_iota(jnp.int32, (n, n), 0) < lax.broadcasted_iota(jnp.int32, (n, n), 1)
    ).astype(BF16)
    ids = lax.broadcasted_iota(jnp.int32, (128, n), 0)
    count = jnp.zeros((128, 1), F32)
    for r in range(16):
        owner = jnp.concatenate([owner_ref[k : k + 1, :] for k in (2 * r, 2 * r + 1)], axis=1)
        hit = ids == owner
        one_hot = hit.astype(F32)
        earlier = jnp.dot(one_hot.astype(BF16), before, preferred_element_type=F32) + count
        slot = jnp.sum(one_hot * earlier, axis=0, keepdims=True).astype(jnp.int32)
        count = count + jnp.sum(one_hot, axis=1, keepdims=True)
        apart = (owner >> 5) ^ (group >> 1)
        row = (apart * 16 + (owner & 15)) * 64 + slot
        row = jnp.where(((owner >> 4) & 1) == (group & 1), row, 4096)
        dest_ref[2 * r : 2 * r + 1, :] = row[:, 0:128]
        dest_ref[2 * r + 1 : 2 * r + 2, :] = row[:, 128:256]


def place_kernel(dest_ref, flag_ref, coef_ref, own_late, own_early, core_late, core_early, *refs):
    outs = refs[0:4]
    low_ref, high_ref, packed = refs[4:7]
    group = lax.axis_index("grid")
    w0 = (coef_ref[group] * (1 - flag_ref[group])).astype(F32)
    w1 = (coef_ref[group ^ 1] * (1 - flag_ref[group ^ 1])).astype(F32)

    def add(i, own, core):
        p = w0 * own.astype(F32) + w1 * core.astype(F32)
        low_ref[pl.ds(i * 128, 128), :] = p[:, 0:128]
        high_ref[pl.ds(i * 128, 128), :] = p[:, 128:256]

    for j, i in enumerate(PIECES[0]):
        add(i, own_late[j], core_late[j])
    for i in range(2, 14):
        add(i, own_early[i - 2], core_early[i - 2])
    packed[...] = jnp.zeros_like(packed)

    def step(t, carry):
        base = pl.multiple_of(t * 64, 64)
        for u in range(64):
            packed[pl.ds(dest_ref[2 * base + 2 * u], 1), :] = low_ref[pl.ds(base + u, 1), :]
            packed[pl.ds(dest_ref[2 * base + 2 * u + 1], 1), :] = high_ref[pl.ds(base + u, 1), :]
        return carry

    lax.fori_loop(0, 32, step, 0)
    for q in range(4):
        outs[q][...] = packed[pl.ds(q * 1024, 1024), :].astype(BF16).reshape(16, 64, 128)


def reach(gap_ref, group, other):
    gx, gy = (jnp.maximum(gap_ref[k, group], gap_ref[k, other]) for k in (0, 1))
    rx = jnp.minimum(gx, 2)
    ry = jnp.minimum(gy, 2 - rx)
    return rx, ry, 2 - rx - ry


def picks(length, full_dim, part, skip):
    pos = lax.broadcasted_iota(jnp.int32, (length, length), full_dim) + 1
    place = lax.broadcasted_iota(jnp.int32, (length, length), 1 - full_dim) + 1
    hit = place == part * (length >> skip) + (pos >> skip)
    return jnp.where(hit & kept(pos, skip), 1.0, 0.0).astype(BF16)


def cases(gap_ref, group, other, work):
    rx, ry, _ = reach(gap_ref, group, other)
    for cx in range(3):
        for cy in range(3 - cx):

            @pl.when((rx == cx) & (ry == cy))
            def _():
                work(cx, cy, 2 - cx - cy)


def pack_kernel(gap_ref, partner_ref, late_ref, early_ref, near_ref, far_ref):
    group = lax.axis_index("grid")

    def row(i):
        return early_ref[i - 2] if 2 <= i < 14 else late_ref[PIECES[0].index(i)]

    for m, out_ref in ((1, near_ref), (2, far_ref)):
        target = group ^ (2 * m)

        def work(rx, ry, rz):
            across = [picks(256, 0, part, rz) for part in range(1 << rz)]
            down = [picks(128, 1, part, ry) for part in range(1 << ry)]
            for slab in range(4):
                runs = []
                for y in range(1 << ry):
                    first = (slab << (2 - rx)) + y
                    rows = [row(((first + (z << ry) + 1) << rx) - 1) for z in range(1 << rz)]
                    if rz:
                        hits = [jnp.dot(r, a, preferred_element_type=F32) for r, a in zip(rows, across)]
                        runs.append(sum(hits[1:], hits[0]).astype(BF16))
                    else:
                        runs.append(rows[0])
                if ry:
                    hits = [jnp.dot(d, r, preferred_element_type=F32) for d, r in zip(down, runs)]
                    out_ref[slab] = sum(hits[1:], hits[0]).astype(BF16)
                else:
                    out_ref[slab] = runs[0]

        @pl.when(partner_ref[target] == group)
        def _():
            cases(gap_ref, group, target, work)

        @pl.when(partner_ref[target] != group)
        def _():
            out_ref[...] = jnp.zeros_like(out_ref)


def diff_kernel(gap_ref, partner_ref, own_late, own_early, core_late, core_early, *refs):
    near_ref, far_ref, out_ref, came_ref = refs
    group = lax.axis_index("grid")
    domain = lax.axis_index("dom")
    other = partner_ref[group]
    gx, gy, gz = (jnp.maximum(gap_ref[k, group], gap_ref[k, other]) for k in range(3))
    dims = (128, 256)
    keep_y = kept(lax.broadcasted_iota(jnp.int32, dims, 0) + 1, gy)
    keep_z = kept(lax.broadcasted_iota(jnp.int32, dims, 1) + 1, gz)
    keep = jnp.where(keep_y & keep_z, 1.0, 0.0)
    flip = (other ^ group) >> 1

    def here(i):
        return jnp.where(kept(domain * 16 + (i + 5), gx), 1.0, 0.0)

    def own(i):
        return own_early[i - 2] if 2 <= i < 14 else own_late[PIECES[0].index(i)]

    def core(i):
        return core_early[i - 2] if 2 <= i < 14 else core_late[PIECES[0].index(i)]

    def work(rx, ry, rz):
        across = [picks(256, 1, part, rz) for part in range(1 << rz)]
        down = [picks(128, 0, part, ry) for part in range(1 << ry)]
        for i in range(16):
            if (i + 1) % (1 << rx):
                out_ref[0, i] = jnp.zeros(dims, F32)
                continue
            n = ((i + 1) >> rx) - 1
            sub = n % (1 << (2 - rx))
            theirs = came_ref[n >> (2 - rx)]
            if ry:
                theirs = jnp.dot(down[sub % (1 << ry)], theirs, preferred_element_type=F32)
            if rz:
                theirs = jnp.dot(theirs.astype(BF16), across[sub >> ry], preferred_element_type=F32)
            out_ref[0, i] = (keep * here(i)) * (own(i).astype(F32) - theirs.astype(F32))

    @pl.when(flip == 0)
    def _():
        for i in range(16):
            out_ref[0, i] = (keep * here(i)) * (own(i).astype(F32) - core(i).astype(F32))

    for kind, ref in ((1, near_ref), (2, far_ref)):

        @pl.when(flip == kind)
        def _():
            came_ref[...] = ref[...]

    @pl.when(flip != 0)
    def _():
        cases(gap_ref, group, other, work)


def route_kernel(partner_ref, r0, r1, r2, r3, m1, m2, m3):
    group = lax.axis_index("grid")
    held = (r0, r1, r2, r3)
    for m, out in ((1, m1), (2, m2), (3, m3)):
        target = group ^ (2 * m)
        far = ((partner_ref[target] ^ target) >> 1) == 2

        @pl.when(far)
        def _():
            out[...] = held[m ^ 2][...]

        @pl.when(jnp.logical_not(far))
        def _():
            out[...] = held[m ^ 1][...]


def relayed_diff_kernel(gap_ref, partner_ref, own_late, own_early, core_late, core_early, *refs):
    near, far = refs[0:4], refs[4:8]
    out_ref = refs[8]
    group = lax.axis_index("grid")
    domain = lax.axis_index("dom")
    other = partner_ref[group]
    gx, gy, gz = (jnp.maximum(gap_ref[k, group], gap_ref[k, other]) for k in range(3))
    dims = (128, 256)
    keep_y = kept(lax.broadcasted_iota(jnp.int32, dims, 0) + 1, gy)
    keep_z = kept(lax.broadcasted_iota(jnp.int32, dims, 1) + 1, gz)
    keep = jnp.where(keep_y & keep_z, 1.0, 0.0)
    flip = (other ^ group) >> 1

    def write(theirs):
        for q in range(4):
            for j, i in enumerate(PIECES[q]):
                own = own_early[i - 2] if q else own_late[j]
                here = keep * jnp.where(kept(domain * 16 + (i + 5), gx), 1.0, 0.0)
                out_ref[0, i] = here * (own.astype(F32) - theirs(q, j, i).astype(F32))

    @pl.when(flip == 0)
    def _():
        write(lambda q, j, i: core_early[i - 2] if q else core_late[j])

    @pl.when(flip == 1)
    def _():
        write(lambda q, j, i: near[q][j])

    @pl.when(flip == 2)
    def _():
        write(lambda q, j, i: far[q][j])


def head_kernel(field_hbm, gap_hbm, partner_hbm, fits_ref, first_hbm, second_hbm, gap_ref, partner_ref, sems):
    odd = lax.axis_index("dom") % 2
    copies = [
        pltpu.make_async_copy(gap_hbm, gap_ref, sems.at[0]),
        pltpu.make_async_copy(partner_hbm, partner_ref, sems.at[1]),
        pltpu.make_async_copy(field_hbm.at[0, 15 - 12 * odd], first_hbm.at[0], sems.at[2]),
        pltpu.make_async_copy(field_hbm.at[0, 3 + 12 * odd], second_hbm.at[0], sems.at[3]),
    ]
    for copy in copies:
        copy.start()
    for copy in copies[:2]:
        copy.wait()
    fits = jnp.int32(1)
    for group in range(8):
        other = partner_ref[group]
        skips = jnp.int32(0)
        for k in range(3):
            skips = skips + jnp.maximum(gap_ref[k, group], gap_ref[k, other])
        fits = jnp.where((other != (group ^ 1)) & (skips < 2), 0, fits)
    fits_ref[0] = fits
    for copy in copies[2:]:
        copy.wait()


def sum_kernel(p0, p1, p2, p3, out_ref):
    total = (p0[...].astype(F32) + p1[...].astype(F32)) + (p2[...].astype(F32) + p3[...].astype(F32))
    for rank, k in enumerate(ORDER):
        out_ref[rank] = total[k].astype(BF16)


def owned_kernel(came_ref, out_ref):
    for rank, k in enumerate(ORDER):
        out_ref[0, k] = came_ref[rank].astype(F32)


def call(kernel, outs, ins, scratch=(), flops=0, nbytes=1 << 20, name=None):
    many = isinstance(outs, (list, tuple))
    return pl.pallas_call(
        kernel,
        out_shape=outs,
        in_specs=ins,
        out_specs=[vmem() for _ in outs] if many else vmem(),
        scratch_shapes=scratch,
        compiler_params=params(),
        cost_estimate=cost(flops, nbytes),
        name=name,
    )


def flipped(value, axis, bits):
    return lax.ppermute(value, axis, [(i, i ^ bits) for i in range(lax.axis_size(axis))])


def program(small, first, second, nodal, gaps, partner, flags, coefs, owners):
    one = flipped(first, "dom", 1)
    two = lax.ppermute(
        second, "dom", [(i, i + 1) for i in range(1, 15, 2)] + [(i + 1, i) for i in range(1, 15, 2)]
    )

    piece = shape((4, 128, 256), BF16)
    inner = shape((12, 128, 256), BF16)
    early, *pieces = call(
        early_kernel, [inner] + [piece] * (0 if small else 3), [smem(), vmem(), anywhere()],
        flops=10**9, nbytes=2 << 20, name="early",
    )(gaps, nodal, second)
    early, one, two = lax.optimization_barrier((early, one, two))
    core_early = flipped(early, "grid", 1)
    dest = call(slots_kernel, shape((32, 128), jnp.int32), [vmem()], flops=10**9, name="slots")(
        owners.reshape(32, 128)
    ).reshape(4096)
    late = call(late_kernel, piece, [smem()] + [vmem()] * 3,
                flops=10**9, name="late")(gaps, nodal, one, two)
    core_late = flipped(late, "grid", 1)
    held = (late, early, core_late, core_early)

    bundle = shape((16, 64, 128), BF16)
    packed = call(
        place_kernel, [bundle] * 4, [smem()] * 3 + [vmem()] * 4,
        scratch=[pltpu.VMEM((2048, 128), F32), pltpu.VMEM((2048, 128), F32), pltpu.VMEM((4104, 128), F32)],
        flops=10**7, nbytes=16 << 20, name="place",
    )(dest, flags, coefs, *held)
    summed = [packed[0]] + [flipped(packed[b], "grid", 2 * b) for b in (2, 3, 1)]

    if small:
        near, far = call(
            pack_kernel, [piece] * 2, [smem(), smem(), vmem(), vmem()],
            flops=10**9, nbytes=2 << 20, name="pack",
        )(gaps, partner, late, early)
        far = flipped(far, "grid", 4)
        theirs = (flipped(near, "grid", 2), far)
    else:
        got = [late] + [flipped(pieces[b - 1], "grid", 2 * b) for b in (1, 2, 3)]
        sent = call(route_kernel, [piece] * 3, [smem()] + [vmem()] * 4, name="route")(partner, *got)
        came = [None] + [flipped(sent[m - 1], "grid", 2 * m) for m in (1, 2, 3)]
        theirs = (came[1], got[1], came[3], came[2], came[2], came[3], got[2], came[1])

    total = call(sum_kernel, bundle, [vmem()] * 4, name="sum")(*summed)
    moved = lax.all_to_all(total, "dom", 0, 0, tiled=True, axis_index_groups=[ORDER])
    owned = call(owned_kernel, shape((1, 16, 64, 128), F32), [vmem()], name="owned")(moved)

    diff = call(
        diff_kernel if small else relayed_diff_kernel, shape((1, 16, 128, 256), F32),
        [smem()] * 2 + [vmem()] * (4 + len(theirs)),
        scratch=[pltpu.VMEM((4, 128, 256), BF16)] if small else (), nbytes=6 << 20, name="diff",
    )(gaps, partner, *held, *theirs)
    return diff, owned


def body(nodal, level_gap, partner, flags, coefs, owners):
    gaps = level_gap.T
    edge = shape((1, 128, 256), BF16)
    fits, first, second = pl.pallas_call(
        head_kernel,
        out_shape=[shape((1,), jnp.int32), edge, edge],
        in_specs=[anywhere()] * 3,
        out_specs=[smem(), anywhere(), anywhere()],
        scratch_shapes=[
            pltpu.SMEM((3, 8), jnp.int32), pltpu.SMEM((8,), jnp.int32), pltpu.SemaphoreType.DMA((4,))
        ],
        compiler_params=pltpu.CompilerParams(vmem_limit_bytes=8 * 1024 * 1024),
        name="head",
    )(nodal, gaps, partner)
    return lax.cond(
        fits[0] != 0,
        functools.partial(program, True),
        functools.partial(program, False),
        first, second, nodal, gaps, partner, flags, coefs, owners,
    )


def solution(mesh):
    in_specs = (P("grid", "dom", None, None), P(), P(), P(), P(), P("dom", None))
    out_specs = (P("grid", "dom", None, None), P(("grid", "dom"), None, None, None))
    return jax.shard_map(body, mesh=mesh, in_specs=in_specs, out_specs=out_specs, check_vma=False)
```
